32 devices in a mesh: row: 2 (over y), col: 16 (over z, x, core).
Axes of the slice: x: 2, y: 2, z: 4, core: 2. Of those that a mesh axis runs over, the one named last changes fastest.
Arguments:
- alignment: float32 [128, 384, 256], P('row', 'col'), may hold values from -40 to 40
- seq_mask: int32 [128], replicated, may hold values 0 or 1
- res_mask: int32 [384], replicated, may hold values 0 or 1
- attn_gain: float32 [256], replicated, may hold values from 0.5 to 1.5
- outer_product_gain: float32 [256], replicated, may hold values from 0.5 to 1.5
- w_query: bfloat16 [256, 256], replicated, may hold values from -24 to 24
- w_key: bfloat16 [256, 256], replicated, may hold values from -2 to 2
- w_value: bfloat16 [256, 256], replicated, may hold values from -0.375 to 0.375
- w_gate: bfloat16 [256, 256], replicated, may hold values from -0.375 to 0.375
- output_weight: bfloat16 [256, 256], replicated, may hold values from -0.375 to 0.375
- w_left: bfloat16 [256, 32], replicated, may hold values from -0.375 to 0.375
- w_right: bfloat16 [256, 32], replicated, may hold values from -0.375 to 0.375
- w_pair: bfloat16 [1024, 128], replicated, may hold values from -3 to 3
Outputs:
- alignment_output: float32 [128, 384, 256], P('row', 'col')
- pair_increment: float32 [384, 384, 128], P('row', 'col')
The draws below stay inside these ranges and needn't reach their ends.
All inputs are finite; a program needn't handle non-finite values.
Results may differ from the reference program's by a relative error of at most 0.0095.
Values may be sent and summed in bfloat16 or wider, within the bound.
A program may use at most 128 MiB of HBM per device.

```python
import math
import jax
import jax.numpy as jnp
from jax import lax

C = 256
HEADS = 8
HEAD_DIM = 32
COPM = 32
CZ = 128
SEQS = 128
RES = 384


def draw_alignment(key, part):
    normals = jax.random.normal(jax.random.fold_in(key, 1), (SEQS, RES, C), jnp.float32)
    return jnp.clip(normals, -6.0, 6.0)


def key_matrix(key):
    entries = jax.random.normal(jax.random.fold_in(key, 7), (C, HEADS * HEAD_DIM), jnp.float32) / math.sqrt(C)
    return jnp.clip(entries, -6.0 / math.sqrt(C), 6.0 / math.sqrt(C))


def draw_w_key(key, part):
    return key_matrix(key).astype(jnp.bfloat16)


def draw_w_query(key, part):
    independent = key_matrix(jax.random.fold_in(key, 3))
    return independent.astype(jnp.bfloat16)


def touch_ends(array, rng, least, largest):
    place = [jax.random.randint(jax.random.fold_in(rng, axis), (), 0, length) for axis, length in enumerate(array.shape)]
    widest = array.shape.index(max(array.shape))
    neighbour = place[:widest] + [(place[widest] + 1) % array.shape[widest]] + place[widest + 1:]
    return array.at[tuple(place)].set(least).at[tuple(neighbour)].set(largest)


def scatter_about(key, dims, width, limit, kind=jnp.bfloat16):
    values = width * jax.random.normal(key, dims, jnp.float32)
    return jnp.clip(values, min=-limit, max=limit).astype(kind)


def setup_inputs(seed: int = 0) -> dict:
    streams_of = jax.random.split(jax.random.key(seed), 14)
    alignment = draw_alignment(jax.random.fold_in(streams_of[13], 71), 0)
    seq_mask = touch_ends((jax.random.randint(streams_of[1], (SEQS,), 0, 8) < 7).astype(jnp.int32), jax.random.fold_in(streams_of[1], 1), 0, 1)
    res_mask = touch_ends((jax.random.randint(streams_of[2], (RES,), 0, 8) < 7).astype(jnp.int32), jax.random.fold_in(streams_of[2], 1), 0, 1)
    attn_gain = jnp.clip(1.0 + 0.1 * jax.random.normal(streams_of[3], (C,), jnp.float32), 0.5, 1.5)
    outer_product_gain = jnp.clip(1.0 + 0.1 * jax.random.normal(streams_of[4], (C,), jnp.float32), 0.5, 1.5)
    w_query = draw_w_query(jax.random.fold_in(streams_of[13], 71), 0)
    w_key = draw_w_key(jax.random.fold_in(streams_of[13], 71), 0)
    w_value = scatter_about(streams_of[7], (C, HEADS * HEAD_DIM), C ** -0.5, 0.375)
    w_gate = scatter_about(streams_of[8], (C, HEADS * HEAD_DIM), C ** -0.5, 0.375)
    output_weight = scatter_about(streams_of[9], (HEADS * HEAD_DIM, C), (HEADS * HEAD_DIM) ** -0.5, 0.375)
    w_left = scatter_about(streams_of[10], (C, COPM), C ** -0.5, 0.375)
    w_right = scatter_about(streams_of[11], (C, COPM), C ** -0.5, 0.375)
    w_pair = scatter_about(streams_of[12], (COPM * COPM, CZ), 0.5, 3.0)
    return dict(alignment=alignment, seq_mask=seq_mask, res_mask=res_mask, attn_gain=attn_gain, outer_product_gain=outer_product_gain, w_query=w_query, w_key=w_key, w_value=w_value, w_gate=w_gate, output_weight=output_weight, w_left=w_left, w_right=w_right, w_pair=w_pair)


def normalized_rows(values, gains):
    average = lax.optimization_barrier(jnp.mean(values, -1, keepdims=True))
    centred = values - average
    spread = lax.optimization_barrier(jnp.mean(centred * centred, -1, keepdims=True))
    return centred * lax.rsqrt(spread + 1e-05) * gains

def reference(alignment, seq_mask, res_mask, attn_gain, outer_product_gain, w_query, w_key, w_value, w_gate, output_weight, w_left, w_right, w_pair):
    sequence_total, residue_total, channel_width = alignment.shape
    hidden = w_query.shape[1]
    normed = normalized_rows(alignment, attn_gain).astype(jnp.bfloat16).reshape(-1, channel_width)
    query_scale = HEAD_DIM ** (-0.5)
    queries = (jnp.dot(normed, w_query, preferred_element_type=jnp.float32) * query_scale).astype(jnp.bfloat16)
    key_rows = jnp.dot(normed, w_key, preferred_element_type=jnp.float32).astype(jnp.bfloat16)
    value_rows = jnp.dot(normed, w_value, preferred_element_type=jnp.float32).astype(jnp.bfloat16)
    gate_lin = jnp.dot(normed, w_gate, preferred_element_type=jnp.float32)
    key_bias = jnp.where(seq_mask > 0, 0.0, -1000000000.0).astype(jnp.float32)

    def arrange(values):
        return values.reshape(sequence_total, residue_total, -1).transpose(1, 0, 2)

    def column(column_parts):
        col_query, col_key, col_value, col_gate = column_parts
        heads_query = col_query.reshape(sequence_total, HEADS, HEAD_DIM).astype(jnp.float32)
        heads_key = col_key.reshape(sequence_total, HEADS, HEAD_DIM).astype(jnp.float32)
        heads_value = col_value.reshape(sequence_total, HEADS, HEAD_DIM).astype(jnp.float32)
        logits = jnp.einsum('shd,thd->hst', heads_query, heads_key) + key_bias[None, None, :]
        weights = jax.nn.softmax(logits, axis=-1).astype(jnp.bfloat16)
        attended = jnp.einsum('hst,thd->shd', weights.astype(jnp.float32), heads_value).reshape(sequence_total, hidden)
        return (jax.nn.sigmoid(col_gate) * attended).astype(jnp.bfloat16)
    gated_output = lax.map(column, (arrange(queries), arrange(key_rows), arrange(value_rows), arrange(gate_lin)))
    gated_output = gated_output.transpose(1, 0, 2).reshape(-1, hidden)
    alignment_output = alignment + jnp.dot(gated_output, output_weight, preferred_element_type=jnp.float32).reshape(sequence_total, residue_total, channel_width)
    second_normalized = normalized_rows(alignment_output, outer_product_gain).astype(jnp.bfloat16).reshape(-1, channel_width)
    side_mask = (seq_mask[:, None] * res_mask[None, :]).astype(jnp.float32)[:, :, None]
    left = (jnp.dot(second_normalized, w_left, preferred_element_type=jnp.float32).reshape(sequence_total, residue_total, COPM) * side_mask).astype(jnp.bfloat16).reshape(sequence_total, -1)
    right = (jnp.dot(second_normalized, w_right, preferred_element_type=jnp.float32).reshape(sequence_total, residue_total, COPM) * side_mask).astype(jnp.bfloat16).reshape(sequence_total, -1)
    live_total = jnp.sum(seq_mask)
    block_rows = 32
    contraction = (((0,), (0,)), ((), ()))

    def pair_block(offset):
        left_part = lax.dynamic_slice_in_dim(left, (offset * COPM).astype(jnp.int32), block_rows * COPM, 1)
        products = lax.dot_general(left_part, right, contraction, preferred_element_type=jnp.float32)
        outer_sum = products.reshape(block_rows, COPM, residue_total, COPM).transpose(0, 2, 1, 3).reshape(-1, COPM * COPM).astype(jnp.bfloat16)
        projected_output = jnp.dot(outer_sum, w_pair, preferred_element_type=jnp.float32).reshape(block_rows, residue_total, -1)
        block_mask = lax.dynamic_slice_in_dim(res_mask, offset.astype(jnp.int32), block_rows, 0)
        count_values = jnp.maximum(live_total * block_mask[:, None] * res_mask[None, :], 1).astype(jnp.float32)
        return projected_output / count_values[:, :, None]
    offsets = jnp.arange(residue_total // block_rows, dtype=jnp.int32) * block_rows
    pair_increment = lax.map(pair_block, offsets).reshape(residue_total, residue_total, -1)
    return (alignment_output, pair_increment)
```

```python
import functools

import jax
import jax.numpy as jnp
from jax import lax
from jax.experimental import pallas as pl
from jax.experimental.pallas import tpu as pltpu
from jax.sharding import PartitionSpec as P

HEAD_DIM = 32
LANES = 128
CHUNK = 8
BF = jnp.bfloat16
F32 = jnp.float32
VM = pl.BlockSpec(memory_space=pltpu.VMEM)
SM = pl.BlockSpec(memory_space=pltpu.SMEM)
PARAMS = pltpu.CompilerParams(vmem_limit_bytes=60 << 20)


def nt(a, b):
    return lax.dot_general(a, b, (((1,), (1,)), ((), ())), preferred_element_type=F32)


def mm(a, b):
    return jnp.dot(a, b, preferred_element_type=F32)


def norm_rows(values, gains):
    average = jnp.mean(values, -1, keepdims=True)
    centred = values - average
    spread = jnp.mean(centred * centred, -1, keepdims=True)
    return centred * lax.rsqrt(spread + 1e-05) * gains


def norm_kernel(seqs, res, x_ref, g_ref, o_ref):
    gains = g_ref[...]
    for r in range(CHUNK):
        rows = x_ref[:, r, :]
        o_ref[r] = norm_rows(rows, gains).astype(BF)


def norm_chunk(x, gain, chunk):
    seqs, res, width = x.shape
    return pl.pallas_call(
        functools.partial(norm_kernel, seqs, res),
        grid=(1,),
        in_specs=[
            pl.BlockSpec((seqs, CHUNK, width), lambda i: (0, chunk, 0)),
            pl.BlockSpec((1, width), lambda i: (0, 0)),
        ],
        out_specs=pl.BlockSpec((CHUNK, seqs, width), lambda i: (0, 0, 0)),
        out_shape=jax.ShapeDtypeStruct((CHUNK, seqs, width), BF),
        cost_estimate=pl.CostEstimate(flops=1 << 20, bytes_accessed=1 << 20, transcendentals=0),
        compiler_params=PARAMS,
        name="norm",
    )(x, gain)


def attend_kernel(rows_n, aliased, *refs):
    xs = refs[:rows_n]
    x_ref, sm_ref, wq, wk, wv, wg, wo = refs[rows_n : rows_n + 7]
    out_ref, q_s, k_s, v_s, g_s = refs[-5:]
    seqs, width = xs[0].shape[1], xs[0].shape[2]
    total = seqs * rows_n
    hidden = wq.shape[1]
    row = lax.axis_index("row")
    own = xs[0][...].reshape(CHUNK * seqs, width)
    q_s[...] = (mm(own, wq[...]) * (HEAD_DIM**-0.5)).astype(BF).reshape(CHUNK, seqs, hidden)
    g_s[...] = mm(own, wg[...]).reshape(CHUNK, seqs, hidden)
    for d in range(rows_n):
        part = xs[d][...].reshape(CHUNK * seqs, width)
        at = slice(d * seqs, (d + 1) * seqs)
        k_s[:, at, :] = mm(part, wk[...]).astype(BF).reshape(CHUNK, seqs, hidden)
        v_s[:, at, :] = mm(part, wv[...]).astype(BF).reshape(CHUNK, seqs, hidden)
    live = jnp.concatenate(
        [sm_ref[pl.ds(lax.rem(row + d, rows_n), 1), :] for d in range(rows_n)], axis=1
    )
    bias = jnp.where(live > 0, 0.0, -1000000000.0).astype(F32)
    group = LANES // HEAD_DIM
    lane = lax.broadcasted_iota(jnp.int32, (seqs, LANES), 1) // HEAD_DIM
    ones = jnp.ones((total, LANES), BF)
    outs = []
    for r in range(CHUNK):
        halves = []
        for half in range(hidden // LANES):
            at = slice(half * LANES, (half + 1) * LANES)
            q = q_s[r, :, at]
            spread = jnp.concatenate(
                [jnp.where(lane == h, q, jnp.zeros_like(q)) for h in range(group)], axis=0
            )
            logits = nt(spread, k_s[r, :, at]) + bias
            peak = jnp.max(logits, axis=-1, keepdims=True)
            weights = jnp.exp(logits - peak).astype(BF)
            mixed = mm(weights, jnp.concatenate([v_s[r, :, at], ones], axis=1))
            top = mixed[:seqs, :LANES]
            den = mixed[:seqs, LANES:]
            for h in range(1, group):
                part = mixed[h * seqs : (h + 1) * seqs]
                top = jnp.where(lane == h, part[:, :LANES], top)
                den = jnp.where(lane == h, part[:, LANES:], den)
            halves.append((jax.nn.sigmoid(g_s[r, :, at]) * (top / den)).astype(BF))
        outs.append(jnp.concatenate(halves, axis=1))
    projected = mm(jnp.concatenate(outs, axis=0), wo[...])
    for r in range(CHUNK):
        out_ref[:, r, :] = x_ref[:, r, :] + projected[r * seqs : (r + 1) * seqs]


def attend_chunk(parts, x, sm, weights, chunk, previous):
    rows_n = len(parts)
    seqs, res, width = x.shape
    total = seqs * rows_n
    hidden = weights[0].shape[1]

    def whole(a):
        return pl.BlockSpec(a.shape, lambda i: (0,) * a.ndim)

    block = pl.BlockSpec((seqs, CHUNK, width), lambda i: (0, chunk, 0))
    args = [*parts, x, sm, *weights]
    specs = [whole(p) for p in parts] + [block, whole(sm)] + [whole(w) for w in weights]
    alias = {}
    if previous is not None:
        alias = {len(args): 0}
        args.append(previous)
        specs.append(pl.BlockSpec(memory_space=pl.ANY))
    tokens = CHUNK * total
    return pl.pallas_call(
        functools.partial(attend_kernel, rows_n, previous is not None),
        grid=(1,),
        in_specs=specs,
        out_specs=block,
        out_shape=jax.ShapeDtypeStruct(x.shape, F32),
        scratch_shapes=[
            pltpu.VMEM((CHUNK, seqs, hidden), BF),
            pltpu.VMEM((CHUNK, total, hidden), BF),
            pltpu.VMEM((CHUNK, total, hidden), BF),
            pltpu.VMEM((CHUNK, seqs, hidden), F32),
        ],
        input_output_aliases=alias,
        cost_estimate=pl.CostEstimate(
            flops=tokens * width * hidden * 40, bytes_accessed=4 << 20, transcendentals=tokens * 8 * 64
        ),
        compiler_params=PARAMS,
        name="attend",
    )(*args)


def sides_kernel(pad, x_ref, g_ref, sm_ref, rm_ref, w_ref, l_ref, r_ref, l_s):
    seqs, res, width = x_ref.shape
    side = w_ref.shape[0] // 2
    half = side // 2
    row = lax.axis_index("row")
    col = lax.axis_index("col")
    seq_live = sm_ref[pl.ds(row, 1), :].astype(F32)
    gains = g_ref[...]
    l_s[...] = jnp.zeros_like(l_s)
    for r in range(res):
        second = norm_rows(x_ref[:, r, :], gains).astype(BF)
        live = seq_live * rm_ref[col * res + r].astype(F32)
        both = nt(w_ref[...], second) * live
        l_s[:, r, :] = jnp.concatenate([both[:half], both[half:side]], axis=1)
        r_ref[r] = jnp.concatenate([both[side : side + half], both[side + half :]], axis=1).astype(BF)
    l_ref[...] = l_s[...].astype(BF)


def pair_kernel(rows_n, patterns, sizes, *refs):
    count = rows_n * len(sizes)
    l_refs, r_refs = refs[:count], refs[count : count + rows_n]
    sm_ref, rm_ref, rmv_ref, w_ref, out_ref, l_s, r_s, o_s, c_s = refs[count + rows_n :]
    res = r_refs[0].shape[0]
    half = r_refs[0].shape[1]
    side = 2 * half
    pad = l_refs[0].shape[2]
    slots = len(patterns)
    seqs = l_refs[0].shape[3] // 2
    row = lax.axis_index("row")
    col = lax.axis_index("col")
    local = lax.rem(col, slots)

    def halves(parts):
        low = jnp.concatenate([p[..., :seqs] for p in parts], axis=-1)
        high = jnp.concatenate([p[..., seqs:] for p in parts], axis=-1)
        return low, high

    base = 0
    for stage, size in enumerate(sizes):
        for k in range(size):
            at = slice((base + k) * pad, (base + k + 1) * pad)
            low, high = halves([l_refs[stage * rows_n + d][k] for d in range(rows_n)])
            l_s[:half, at, :] = low
            l_s[half:, at, :] = high
        base += size
    low, high = halves([r[...] for r in r_refs])
    r_s[:, :half, :] = low
    r_s[:, half:, :] = high
    live_total = jnp.sum(sm_ref[...])
    pieces = []
    for p in patterns:
        block = row * slots + jnp.bitwise_xor(local, p)
        pieces.append(rmv_ref[pl.ds(block, 1), :])
    c_s[...] = jnp.concatenate(pieces, axis=1)
    step = o_s.shape[0]

    def group(n, carry):
        lhs = r_s[pl.ds(n * step, step)].reshape(step * side, rows_n * seqs)
        for a in range(side):
            block = nt(lhs, l_s[a]).astype(BF)
            o_s[:, a * side : (a + 1) * side, :] = block.reshape(step, side, slots * pad)
        for jj in range(step):
            j = n * step + jj
            live = live_total * rm_ref[col * res + j]
            counts = jnp.maximum(live * c_s[...], 1).astype(F32)
            flat = mm(w_ref[...], o_s[jj]) / counts
            rows = flat.T
            for k, p in enumerate(patterns):
                block = pl.multiple_of(jnp.bitwise_xor(local, p) * res, res)
                out_ref[pl.ds(block, res), j, :] = rows[k * pad : k * pad + res]
        return carry

    lax.fori_loop(0, res // step, group, 0)


def shards(
    alignment, seq_mask, res_mask, attn_gain, outer_product_gain, w_query, w_key, w_value, w_gate,
    output_weight, w_left, w_right, w_pair,
):
    seqs, res, width = alignment.shape
    rows_n = lax.axis_size("row")
    cols_n = lax.axis_size("col")
    slots = cols_n // rows_n
    side = w_left.shape[1]
    half = side // 2
    sm = seq_mask.reshape(rows_n, seqs)
    pad = -(-res // 16) * 16
    gain = attn_gain.reshape(1, width)
    weights = (w_query, w_key, w_value, w_gate, output_weight)
    chunks = res // CHUNK
    parts = []
    for n in range(chunks):
        own = norm_chunk(alignment, gain, n)
        got = [own]
        for d in range(1, rows_n):
            perm = [((r + d) % rows_n, r) for r in range(rows_n)]
            got.append(lax.ppermute(own, "row", perm))
        parts.append(got)
    result = None
    for n in range(chunks):
        result = attend_chunk(parts[n], alignment, sm, weights, n, result)

    w_sides = jnp.concatenate([w_left, w_right], axis=1).T
    left, right = pl.pallas_call(
        functools.partial(sides_kernel, pad),
        in_specs=[VM, VM, VM, SM, VM],
        out_specs=(VM, VM),
        out_shape=(
            jax.ShapeDtypeStruct((half, pad, 2 * seqs), BF),
            jax.ShapeDtypeStruct((res, half, 2 * seqs), BF),
        ),
        scratch_shapes=[pltpu.VMEM((half, pad, 2 * seqs), F32)],
        compiler_params=PARAMS,
        name="sides",
    )(result, outer_product_gain.reshape(1, width), sm, res_mask, w_sides)

    rights = [right]
    for d in range(1, rows_n):
        perm = [((r + d) % rows_n, r) for r in range(rows_n)]
        rights.append(lax.ppermute(right, "row", perm))
    row = lax.axis_index("row")
    shift = lax.rem(lax.axis_index("col") // slots - row + rows_n, rows_n)
    stage = []
    for d in range(rows_n):
        unit = None
        for k in range(rows_n):
            if d == 0 and k == 0:
                got = left
            else:
                perm = [
                    (((r + d) % rows_n) * cols_n + r * slots + g, r * cols_n + ((r + k) % rows_n) * slots + g)
                    for r in range(rows_n)
                    for g in range(slots)
                ]
                got = lax.ppermute(left, ("row", "col"), perm)
            unit = got if unit is None else jnp.where(shift == k, got, unit)
        stage.append(unit[None])
    bits = [1 << n for n in range(slots.bit_length() - 1)]
    bits = bits[1:] + bits[:1]
    patterns = [0]
    sizes = [1]
    stages = [stage]
    for bit in bits:
        perm = [(c, c ^ bit) for c in range(cols_n)]
        fresh = []
        for d in range(rows_n):
            held = [s[d] for s in stages]
            sent = [lax.ppermute(h, "col", perm) for h in held]
            fresh.append(sent)
        patterns = patterns + [p ^ bit for p in patterns]
        for m in range(len(stages)):
            sizes.append(sizes[m])
            stages.append([fresh[d][m] for d in range(rows_n)])
    pair_rows = res * slots
    step = CHUNK
    pair = pl.pallas_call(
        functools.partial(pair_kernel, rows_n, tuple(patterns), tuple(sizes)),
        in_specs=[VM] * (rows_n * len(sizes) + rows_n) + [VM, SM, VM, VM],
        out_specs=VM,
        out_shape=jax.ShapeDtypeStruct((pair_rows, res, w_pair.shape[1]), F32),
        scratch_shapes=[
            pltpu.VMEM((side, slots * pad, rows_n * seqs), BF),
            pltpu.VMEM((res, side, rows_n * seqs), BF),
            pltpu.VMEM((step, side * side, slots * pad), BF),
            pltpu.VMEM((1, slots * pad), jnp.int32),
        ],
        compiler_params=PARAMS,
        name="pairs",
    )(
        *[u for s in stages for u in s], *rights, sm, res_mask,
        jnp.pad(res_mask.reshape(cols_n, res), ((0, 0), (0, pad - res))), w_pair.T,
    )
    return (result, pair)


def solution(mesh):
    in_specs = (P("row", "col", None),) + (P(),) * 12
    out_specs = (P("row", "col", None), P("row", "col", None))
    return jax.shard_map(shards, mesh=mesh, in_specs=in_specs, out_specs=out_specs, check_vma=False)
```

```python
import functools

import jax
import jax.numpy as jnp
from jax import lax
from jax.experimental import pallas as pl
from jax.experimental.pallas import tpu as pltpu
from jax.sharding import PartitionSpec as P

HEAD_DIM = 32
LANES = 128
CHUNK = 8
BF = jnp.bfloat16
F32 = jnp.float32
VM = pl.BlockSpec(memory_space=pltpu.VMEM)
SM = pl.BlockSpec(memory_space=pltpu.SMEM)
PARAMS = pltpu.CompilerParams(vmem_limit_bytes=60 << 20)


def nt(a, b):
    return lax.dot_general(a, b, (((1,), (1,)), ((), ())), preferred_element_type=F32)


def mm(a, b):
    return jnp.dot(a, b, preferred_element_type=F32)


def norm_rows(values, gains):
    average = jnp.mean(values, -1, keepdims=True)
    centred = values - average
    spread = jnp.mean(centred * centred, -1, keepdims=True)
    return centred * lax.rsqrt(spread + 1e-05) * gains


def norm_kernel(seqs, res, x_ref, g_ref, o_ref):
    gains = g_ref[...]
    for r in range(CHUNK):
        rows = x_ref[:, r, :]
        o_ref[r] = norm_rows(rows, gains).astype(BF)


def norm_chunk(x, gain, chunk):
    seqs, res, width = x.shape
    return pl.pallas_call(
        functools.partial(norm_kernel, seqs, res),
        grid=(1,),
        in_specs=[
            pl.BlockSpec((seqs, CHUNK, width), lambda i: (0, chunk, 0)),
            pl.BlockSpec((1, width), lambda i: (0, 0)),
        ],
        out_specs=pl.BlockSpec((CHUNK, seqs, width), lambda i: (0, 0, 0)),
        out_shape=jax.ShapeDtypeStruct((CHUNK, seqs, width), BF),
        cost_estimate=pl.CostEstimate(flops=1 << 20, bytes_accessed=1 << 20, transcendentals=0),
        compiler_params=PARAMS,
        name="norm",
    )(x, gain)


def attend_kernel(rows_n, aliased, *refs):
    xs = refs[:rows_n]
    x_ref, sm_ref, wq, wk, wv, wg, wo = refs[rows_n : rows_n + 7]
    out_ref, q_s, k_s, v_s, g_s = refs[-5:]
    seqs, width = xs[0].shape[1], xs[0].shape[2]
    total = seqs * rows_n
    hidden = wq.shape[1]
    row = lax.axis_index("row")
    own = xs[0][...].reshape(CHUNK * seqs, width)
    q_s[...] = (mm(own, wq[...]) * (HEAD_DIM**-0.5)).astype(BF).reshape(CHUNK, seqs, hidden)
    g_s[...] = mm(own, wg[...]).reshape(CHUNK, seqs, hidden)
    for d in range(rows_n):
        part = xs[d][...].reshape(CHUNK * seqs, width)
        at = slice(d * seqs, (d + 1) * seqs)
        k_s[:, at, :] = mm(part, wk[...]).astype(BF).reshape(CHUNK, seqs, hidden)
        v_s[:, at, :] = mm(part, wv[...]).astype(BF).reshape(CHUNK, seqs, hidden)
    live = jnp.concatenate(
        [sm_ref[pl.ds(lax.rem(row + d, rows_n), 1), :] for d in range(rows_n)], axis=1
    )
    bias = jnp.where(live > 0, 0.0, -1000000000.0).astype(F32)
    group = LANES // HEAD_DIM
    lane = lax.broadcasted_iota(jnp.int32, (seqs, LANES), 1) // HEAD_DIM
    ones = jnp.ones((total, LANES), BF)
    outs = []
    for r in range(CHUNK):
        halves = []
        for half in range(hidden // LANES):
            at = slice(half * LANES, (half + 1) * LANES)
            q = q_s[r, :, at]
            spread = jnp.concatenate(
                [jnp.where(lane == h, q, jnp.zeros_like(q)) for h in range(group)], axis=0
            )
            logits = nt(spread, k_s[r, :, at]) + bias
            peak = jnp.max(logits, axis=-1, keepdims=True)
            weights = jnp.exp(logits - peak).astype(BF)
            mixed = mm(weights, jnp.concatenate([v_s[r, :, at], ones], axis=1))
            top = mixed[:seqs, :LANES]
            den = mixed[:seqs, LANES:]
            for h in range(1, group):
                part = mixed[h * seqs : (h + 1) * seqs]
                top = jnp.where(lane == h, part[:, :LANES], top)
                den = jnp.where(lane == h, part[:, LANES:], den)
            halves.append((jax.nn.sigmoid(g_s[r, :, at]) * (top / den)).astype(BF))
        outs.append(jnp.concatenate(halves, axis=1))
    projected = mm(jnp.concatenate(outs, axis=0), wo[...])
    for r in range(CHUNK):
        out_ref[:, r, :] = x_ref[:, r, :] + projected[r * seqs : (r + 1) * seqs]


def attend_chunk(parts, x, sm, weights, chunk, previous):
    rows_n = len(parts)
    seqs, res, width = x.shape
    total = seqs * rows_n
    hidden = weights[0].shape[1]

    def whole(a):
        return pl.BlockSpec(a.shape, lambda i: (0,) * a.ndim)

    block = pl.BlockSpec((seqs, CHUNK, width), lambda i: (0, chunk, 0))
    args = [*parts, x, sm, *weights]
    specs = [whole(p) for p in parts] + [block, whole(sm)] + [whole(w) for w in weights]
    alias = {}
    if previous is not None:
        alias = {len(args): 0}
        args.append(previous)
        specs.append(pl.BlockSpec(memory_space=pl.ANY))
    tokens = CHUNK * total
    return pl.pallas_call(
        functools.partial(attend_kernel, rows_n, previous is not None),
        grid=(1,),
        in_specs=specs,
        out_specs=block,
        out_shape=jax.ShapeDtypeStruct(x.shape, F32),
        scratch_shapes=[
            pltpu.VMEM((CHUNK, seqs, hidden), BF),
            pltpu.VMEM((CHUNK, total, hidden), BF),
            pltpu.VMEM((CHUNK, total, hidden), BF),
            pltpu.VMEM((CHUNK, seqs, hidden), F32),
        ],
        input_output_aliases=alias,
        cost_estimate=pl.CostEstimate(
            flops=tokens * width * hidden * 40, bytes_accessed=4 << 20, transcendentals=tokens * 8 * 64
        ),
        compiler_params=PARAMS,
        name="attend",
    )(*args)


def sides_kernel(pad, x_ref, g_ref, sm_ref, rm_ref, w_ref, l_ref, r_ref, l_s):
    seqs, res, width = x_ref.shape
    side = w_ref.shape[0] // 2
    half = side // 2
    row = lax.axis_index("row")
    col = lax.axis_index("col")
    seq_live = sm_ref[pl.ds(row, 1), :].astype(F32)
    gains = g_ref[...]
    l_s[...] = jnp.zeros_like(l_s)
    for r in range(res):
        second = norm_rows(x_ref[:, r, :], gains).astype(BF)
        live = seq_live * rm_ref[col * res + r].astype(F32)
        both = nt(w_ref[...], second) * live
        l_s[:, r, :] = jnp.concatenate([both[:half], both[half:side]], axis=1)
        r_ref[r] = jnp.concatenate([both[side : side + half], both[side + half :]], axis=1).astype(BF)
    l_ref[...] = l_s[...].astype(BF)


def gather_kernel(slots, l_ref, r_ref, lo_ref, ro_ref, units, rbuf, send, recv, local):
    rows_n = 2
    half, pad, lanes = l_ref.shape
    seqs = lanes // 2
    row = lax.axis_index("row")
    col = lax.axis_index("col")
    top = col // slots
    g = lax.rem(col, slots)
    zl, x, core = lax.rem(col // 4, 2), lax.rem(col // 2, 2), lax.rem(col, 2)
    fx, fz = 2 * (1 - 2 * x), 4 * (1 - 2 * zl)
    f1 = (1 - core) * fx + core * fz
    f2 = core * fx + (1 - core) * fz
    f3 = 1 - 2 * core
    other = 1 - row
    far = col + slots * (1 - 2 * top)
    mesh = pl.DeviceIdType.MESH
    barrier = pltpu.get_barrier_semaphore()
    partners = [(row, far), (other, col), (row, col + f1), (row, col + f2), (row, col + f3)]
    for p in partners:
        pl.semaphore_signal(barrier, inc=1, device_id=p, device_id_type=mesh)
    pl.semaphore_wait(barrier, len(partners))
    spare = rows_n * slots
    mine = 1 - (top + row - 2 * top * row)
    kept = row * slots + g
    place = mine * kept + (1 - mine) * spare

    def copy(src, dst, n, device):
        return pltpu.make_async_remote_copy(
            src_ref=src, dst_ref=dst, send_sem=send.at[n], recv_sem=recv.at[n],
            device_id=device, device_id_type=mesh,
        )

    def unit(index, n, device):
        return copy(units.at[index], units.at[index], n, device)

    def at(which, shift):
        return (row if which == 0 else other) * slots + g + shift

    first = copy(l_ref, units.at[place], 0, (row, far))
    first.start()
    rights = copy(r_ref, rbuf.at[row], 2, (other, col))
    own = pltpu.make_async_copy(l_ref, units.at[place], local.at[0])
    own.start()
    own_right = pltpu.make_async_copy(r_ref, rbuf.at[row], local.at[1])
    own_right.start()
    across = copy(units.at[spare], units.at[kept], 1, (other, col))
    n1 = [unit(at(w, 0), 3 + w, (row, col + f1)) for w in range(2)]
    n2 = [[unit(at(w, s), 5 + 2 * w + m, (row, col + f2)) for m, s in enumerate((0, f1))] for w in range(2)]
    n3 = [
        [unit(at(w, s), 9 + 4 * w + m, (row, col + f3)) for m, s in enumerate((0, f1, f2, f1 + f2))]
        for w in range(2)
    ]
    own.wait()

    def spread():
        n1[0].start()
        n2[0][0].start()
        n3[0][0].start()

    @pl.when(mine == 1)
    def _():
        spread()

    @pl.when(mine == 0)
    def _():
        across.start()

    rights.start()
    first.wait_recv()

    @pl.when(mine == 1)
    def _():
        across.start()

    @pl.when(mine == 0)
    def _():
        spread()

    across.wait_recv()
    n1[1].start()
    n2[1][0].start()
    n3[1][0].start()
    for w in range(2):
        n1[w].wait_recv()
        n2[w][1].start()
        n3[w][1].start()

    def halves(parts):
        low = jnp.concatenate([p[..., :seqs] for p in parts], axis=-1)
        high = jnp.concatenate([p[..., seqs:] for p in parts], axis=-1)
        return low, high

    def assemble(shift):
        slot = g + shift
        low, high = halves([units[d * slots + slot] for d in range(rows_n)])
        where = pl.ds(pl.multiple_of(slot * pad, pad), pad)
        lo_ref[:half, where, :] = low
        lo_ref[half:, where, :] = high

    assemble(0)
    assemble(f1)
    own_right.wait()
    rights.wait_recv()
    low, high = halves([rbuf[d] for d in range(rows_n)])
    ro_ref[:, :half, :] = low
    ro_ref[:, half:, :] = high
    for m, s in enumerate((f2, f1 + f2)):
        for w in range(2):
            n2[w][m].wait_recv()
            n3[w][2 + m].start()
        assemble(s)
    for m, s in enumerate((0, f2, f1, f1 + f2)):
        for w in range(2):
            n3[w][m].wait_recv()
        assemble(f3 + s)
    for c in [first, across, rights, *n1, *n2[0], *n2[1], *n3[0], *n3[1]]:
        c.wait_send()


def gather_sides(left, right, slots):
    half, pad, lanes = left.shape
    res = right.shape[0]
    return pl.pallas_call(
        functools.partial(gather_kernel, slots),
        in_specs=[VM, VM],
        out_specs=(VM, VM),
        out_shape=(
            jax.ShapeDtypeStruct((2 * half, slots * pad, lanes), BF),
            jax.ShapeDtypeStruct((res, 2 * half, lanes), BF),
        ),
        scratch_shapes=[
            pltpu.VMEM((2 * slots + 1, half, pad, lanes), BF),
            pltpu.VMEM((2, res, half, lanes), BF),
            pltpu.SemaphoreType.DMA((17,)),
            pltpu.SemaphoreType.DMA((17,)),
            pltpu.SemaphoreType.DMA((2,)),
        ],
        compiler_params=pltpu.CompilerParams(
            vmem_limit_bytes=60 << 20, collective_id=0, has_side_effects=True
        ),
        name="gather",
    )(left, right)


def join_kernel(rows_n, sizes, *refs):
    count = rows_n * len(sizes)
    l_refs, r_refs = refs[:count], refs[count : count + rows_n]
    lo_ref, ro_ref = refs[count + rows_n :]
    half, pad, lanes = l_refs[0].shape[1:]
    seqs = lanes // 2

    def halves(parts):
        low = jnp.concatenate([p[..., :seqs] for p in parts], axis=-1)
        high = jnp.concatenate([p[..., seqs:] for p in parts], axis=-1)
        return low, high

    base = 0
    for stage, size in enumerate(sizes):
        for k in range(size):
            at = slice((base + k) * pad, (base + k + 1) * pad)
            low, high = halves([l_refs[stage * rows_n + d][k] for d in range(rows_n)])
            lo_ref[:half, at, :] = low
            lo_ref[half:, at, :] = high
        base += size
    low, high = halves([r[...] for r in r_refs])
    ro_ref[:, :half, :] = low
    ro_ref[:, half:, :] = high


def pair_kernel(patterns, l_s, r_s, sm_ref, rm_ref, rmv_ref, w_ref, out_ref, o_s, c_s):
    res, side, depth = r_s.shape
    slots = out_ref.shape[0] // res
    pad = l_s.shape[1] // slots
    row = lax.axis_index("row")
    col = lax.axis_index("col")
    local = lax.rem(col, slots)
    blocks = range(slots) if patterns is None else [jnp.bitwise_xor(local, p) for p in patterns]
    live_total = jnp.sum(sm_ref[...])
    pieces = [rmv_ref[pl.ds(row * slots + b, 1), :] for b in blocks]
    c_s[...] = jnp.concatenate(pieces, axis=1)
    step = o_s.shape[0]

    def group(n, carry):
        lhs = r_s[pl.ds(n * step, step)].reshape(step * side, depth)
        for a in range(side):
            block = nt(lhs, l_s[a]).astype(BF)
            o_s[:, a * side : (a + 1) * side, :] = block.reshape(step, side, slots * pad)
        for jj in range(step):
            j = n * step + jj
            live = live_total * rm_ref[col * res + j]
            counts = jnp.maximum(live * c_s[...], 1).astype(F32)
            flat = mm(w_ref[...], o_s[jj]) / counts
            rows = flat.T
            for k, b in enumerate(blocks):
                where = pl.ds(b * res if patterns is None else pl.multiple_of(b * res, res), res)
                out_ref[where, j, :] = rows[k * pad : k * pad + res]
        return carry

    lax.fori_loop(0, res // step, group, 0)


def shards(
    alignment, seq_mask, res_mask, attn_gain, outer_product_gain, w_query, w_key, w_value, w_gate,
    output_weight, w_left, w_right, w_pair,
):
    seqs, res, width = alignment.shape
    rows_n = lax.axis_size("row")
    cols_n = lax.axis_size("col")
    slots = cols_n // rows_n
    side = w_left.shape[1]
    half = side // 2
    sm = seq_mask.reshape(rows_n, seqs)
    pad = -(-res // 16) * 16
    gain = attn_gain.reshape(1, width)
    weights = (w_query, w_key, w_value, w_gate, output_weight)
    chunks = res // CHUNK
    parts = []
    for n in range(chunks):
        own = norm_chunk(alignment, gain, n)
        got = [own]
        for d in range(1, rows_n):
            perm = [((r + d) % rows_n, r) for r in range(rows_n)]
            got.append(lax.ppermute(own, "row", perm))
        parts.append(got)
    result = None
    for n in range(chunks):
        result = attend_chunk(parts[n], alignment, sm, weights, n, result)

    w_sides = jnp.concatenate([w_left, w_right], axis=1).T
    left, right = pl.pallas_call(
        functools.partial(sides_kernel, pad),
        in_specs=[VM, VM, VM, SM, VM],
        out_specs=(VM, VM),
        out_shape=(
            jax.ShapeDtypeStruct((half, pad, 2 * seqs), BF),
            jax.ShapeDtypeStruct((res, half, 2 * seqs), BF),
        ),
        scratch_shapes=[pltpu.VMEM((half, pad, 2 * seqs), F32)],
        compiler_params=PARAMS,
        name="sides",
    )(result, outer_product_gain.reshape(1, width), sm, res_mask, w_sides)

    pair_rows = res * slots
    if rows_n == 2 and slots == 8:
        patterns = None
        left_all, right_all = gather_sides(left, right, slots)
    else:
        rights = [right]
        for d in range(1, rows_n):
            perm = [((r + d) % rows_n, r) for r in range(rows_n)]
            rights.append(lax.ppermute(right, "row", perm))
        row = lax.axis_index("row")
        shift = lax.rem(lax.axis_index("col") // slots - row + rows_n, rows_n)
        stage = []
        for d in range(rows_n):
            unit = None
            for k in range(rows_n):
                if d == 0 and k == 0:
                    got = left
                else:
                    perm = [
                        (((r + d) % rows_n) * cols_n + r * slots + g, r * cols_n + ((r + k) % rows_n) * slots + g)
                        for r in range(rows_n)
                        for g in range(slots)
                    ]
                    got = lax.ppermute(left, ("row", "col"), perm)
                unit = got if unit is None else jnp.where(shift == k, got, unit)
            stage.append(unit[None])
        bits = [1 << n for n in range(slots.bit_length() - 1)]
        bits = bits[1:] + bits[:1]
        patterns = [0]
        sizes = [1]
        stages = [stage]
        for bit in bits:
            perm = [(c, c ^ bit) for c in range(cols_n)]
            fresh = []
            for d in range(rows_n):
                held = [s[d] for s in stages]
                sent = [lax.ppermute(h, "col", perm) for h in held]
                fresh.append(sent)
            patterns = patterns + [p ^ bit for p in patterns]
            for m in range(len(stages)):
                sizes.append(sizes[m])
                stages.append([fresh[d][m] for d in range(rows_n)])
        patterns = tuple(patterns)
        left_all, right_all = pl.pallas_call(
            functools.partial(join_kernel, rows_n, tuple(sizes)),
            in_specs=[VM] * (rows_n * len(sizes) + rows_n),
            out_specs=(VM, VM),
            out_shape=(
                jax.ShapeDtypeStruct((side, slots * pad, rows_n * seqs), BF),
                jax.ShapeDtypeStruct((res, side, rows_n * seqs), BF),
            ),
            compiler_params=PARAMS,
            name="join",
        )(*[u for s in stages for u in s], *rights)
    pair = pl.pallas_call(
        functools.partial(pair_kernel, patterns),
        in_specs=[VM, VM, VM, SM, VM, VM],
        out_specs=VM,
        out_shape=jax.ShapeDtypeStruct((pair_rows, res, w_pair.shape[1]), F32),
        scratch_shapes=[
            pltpu.VMEM((CHUNK, side * side, slots * pad), BF),
            pltpu.VMEM((1, slots * pad), jnp.int32),
        ],
        compiler_params=PARAMS,
        name="pairs",
    )(
        left_all, right_all, sm, res_mask,
        jnp.pad(res_mask.reshape(cols_n, res), ((0, 0), (0, pad - res))), w_pair.T,
    )
    return (result, pair)


def solution(mesh):
    in_specs = (P("row", "col", None),) + (P(),) * 12
    out_specs = (P("row", "col", None), P("row", "col", None))
    return jax.shard_map(shards, mesh=mesh, in_specs=in_specs, out_specs=out_specs, check_vma=False)
```

```python
import functools

import jax
import jax.numpy as jnp
from jax import lax
from jax.experimental import pallas as pl
from jax.experimental.pallas import tpu as pltpu
from jax.sharding import PartitionSpec as P

HEAD_DIM = 32
LANES = 128
CHUNK = 8
BF = jnp.bfloat16
F32 = jnp.float32
VM = pl.BlockSpec(memory_space=pltpu.VMEM)
SM = pl.BlockSpec(memory_space=pltpu.SMEM)


def params(mib):
    return pltpu.CompilerParams(vmem_limit_bytes=mib << 20)


def pick(mask, index, width, count):
    value = mask[:, :width]
    for d in range(1, count):
        value = jnp.where(index == d, mask[:, d * width : (d + 1) * width], value)
    return value


def nt(a, b):
    return lax.dot_general(a, b, (((1,), (1,)), ((), ())), preferred_element_type=F32)


def mm(a, b):
    return jnp.dot(a, b, preferred_element_type=F32)


def norm_rows(values, gains):
    average = jnp.mean(values, -1, keepdims=True)
    centred = values - average
    spread = jnp.mean(centred * centred, -1, keepdims=True)
    return centred * lax.rsqrt(spread + 1e-05) * gains


def norm_kernel(seqs, res, x_ref, g_ref, o_ref):
    gains = g_ref[...]
    for r in range(CHUNK):
        rows = x_ref[:, r, :]
        o_ref[r] = norm_rows(rows, gains).astype(BF)


def norm_chunk(x, gain, chunk):
    seqs, res, width = x.shape
    return pl.pallas_call(
        functools.partial(norm_kernel, seqs, res),
        grid=(1,),
        in_specs=[
            pl.BlockSpec((seqs, CHUNK, width), lambda i: (0, chunk, 0)),
            pl.BlockSpec((1, width), lambda i: (0, 0)),
        ],
        out_specs=pl.BlockSpec((CHUNK, seqs, width), lambda i: (0, 0, 0)),
        out_shape=jax.ShapeDtypeStruct((CHUNK, seqs, width), BF),
        cost_estimate=pl.CostEstimate(flops=1 << 20, bytes_accessed=1 << 20, transcendentals=0),
        compiler_params=params(4),
        name="norm",
    )(x, gain)


def attend_kernel(rows_n, aliased, *refs):
    xs = refs[:rows_n]
    x_ref, sm_ref, wq, wk, wv, wg, wo = refs[rows_n : rows_n + 7]
    out_ref, q_s, k_s, v_s, g_s = refs[-5:]
    seqs, width = xs[0].shape[1], xs[0].shape[2]
    total = seqs * rows_n
    hidden = wq.shape[1]
    row = lax.axis_index("row")
    own = xs[0][...].reshape(CHUNK * seqs, width)
    q_s[...] = (mm(own, wq[...]) * (HEAD_DIM**-0.5)).astype(BF).reshape(CHUNK, seqs, hidden)
    g_s[...] = mm(own, wg[...]).reshape(CHUNK, seqs, hidden)
    for d in range(rows_n):
        part = xs[d][...].reshape(CHUNK * seqs, width)
        at = slice(d * seqs, (d + 1) * seqs)
        k_s[:, at, :] = mm(part, wk[...]).astype(BF).reshape(CHUNK, seqs, hidden)
        v_s[:, at, :] = mm(part, wv[...]).astype(BF).reshape(CHUNK, seqs, hidden)
    live = jnp.concatenate(
        [pick(sm_ref[...], lax.rem(row + d, rows_n), seqs, rows_n) for d in range(rows_n)], axis=1
    )
    bias = jnp.where(live > 0, 0.0, -1000000000.0).astype(F32)
    group = LANES // HEAD_DIM
    lane = lax.broadcasted_iota(jnp.int32, (seqs, LANES), 1) // HEAD_DIM
    ones = jnp.ones((total, LANES), BF)
    outs = []
    for r in range(CHUNK):
        halves = []
        for half in range(hidden // LANES):
            at = slice(half * LANES, (half + 1) * LANES)
            q = q_s[r, :, at]
            spread = jnp.concatenate(
                [jnp.where(lane == h, q, jnp.zeros_like(q)) for h in range(group)], axis=0
            )
            logits = nt(spread, k_s[r, :, at]) + bias
            peak = jnp.max(logits, axis=-1, keepdims=True)
            weights = jnp.exp(logits - peak).astype(BF)
            mixed = mm(weights, jnp.concatenate([v_s[r, :, at], ones], axis=1))
            top = mixed[:seqs, :LANES]
            den = mixed[:seqs, LANES:]
            for h in range(1, group):
                part = mixed[h * seqs : (h + 1) * seqs]
                top = jnp.where(lane == h, part[:, :LANES], top)
                den = jnp.where(lane == h, part[:, LANES:], den)
            halves.append((jax.nn.sigmoid(g_s[r, :, at]) * (top / den)).astype(BF))
        outs.append(jnp.concatenate(halves, axis=1))
    projected = mm(jnp.concatenate(outs, axis=0), wo[...])
    for r in range(CHUNK):
        out_ref[:, r, :] = x_ref[:, r, :] + projected[r * seqs : (r + 1) * seqs]


def attend_chunk(parts, x, sm, weights, chunk, previous):
    rows_n = len(parts)
    seqs, res, width = x.shape
    total = seqs * rows_n
    hidden = weights[0].shape[1]

    def whole(a):
        return VM

    block = pl.BlockSpec((seqs, CHUNK, width), lambda i: (0, chunk, 0))
    args = [*parts, x, sm, *weights]
    specs = [whole(p) for p in parts] + [block, whole(sm)] + [whole(w) for w in weights]
    alias = {}
    if previous is not None:
        alias = {len(args): 0}
        args.append(previous)
        specs.append(pl.BlockSpec(memory_space=pl.ANY))
    tokens = CHUNK * total
    return pl.pallas_call(
        functools.partial(attend_kernel, rows_n, previous is not None),
        grid=(1,),
        in_specs=specs,
        out_specs=block,
        out_shape=jax.ShapeDtypeStruct(x.shape, F32),
        scratch_shapes=[
            pltpu.VMEM((CHUNK, seqs, hidden), BF),
            pltpu.VMEM((CHUNK, total, hidden), BF),
            pltpu.VMEM((CHUNK, total, hidden), BF),
            pltpu.VMEM((CHUNK, seqs, hidden), F32),
        ],
        input_output_aliases=alias,
        cost_estimate=pl.CostEstimate(
            flops=tokens * width * hidden * 40, bytes_accessed=4 << 20, transcendentals=tokens * 8 * 64
        ),
        compiler_params=params(18 if rows_n == 2 else 48),
        name="attend",
    )(*args)


def sides_kernel(rows_n, x_ref, g_ref, sm_ref, rm_ref, wl_ref, wr_ref, l_ref, r_ref, l_s):
    seqs, res, width = x_ref.shape
    side = wl_ref.shape[0]
    half = side // 2
    row = lax.axis_index("row")
    col = lax.axis_index("col")
    seq_live = pick(sm_ref[...], row, seqs, rows_n).astype(F32)
    gains = g_ref[...]
    weights = jnp.concatenate([wl_ref[...], wr_ref[...]], axis=0)
    for r in range(res):
        second = norm_rows(x_ref[:, r, :], gains).astype(BF)
        live = seq_live * rm_ref[col * res + r].astype(F32)
        both = nt(weights, second) * live
        l_s[:, r, :] = jnp.concatenate([both[:half], both[half:side]], axis=1)
        r_ref[r] = jnp.concatenate([both[side : side + half], both[side + half :]], axis=1).astype(BF)
    l_ref[...] = l_s[...].astype(BF)


def gather_kernel(slots, pad, l_ref, r_ref, lo_ref, ro_ref, units, rbuf, send, recv, local):
    rows_n = 2
    half, res, lanes = l_ref.shape
    seqs = lanes // 2
    row = lax.axis_index("row")
    col = lax.axis_index("col")
    top = col // slots
    g = lax.rem(col, slots)
    zl, x, core = lax.rem(col // 4, 2), lax.rem(col // 2, 2), lax.rem(col, 2)
    fx, fz = 2 * (1 - 2 * x), 4 * (1 - 2 * zl)
    f1 = (1 - core) * fx + core * fz
    f2 = core * fx + (1 - core) * fz
    f3 = 1 - 2 * core
    other = 1 - row
    far = col + slots * (1 - 2 * top)
    mesh = pl.DeviceIdType.MESH
    barrier = pltpu.get_barrier_semaphore()
    partners = [(row, far), (other, col), (row, col + f1), (row, col + f2), (row, col + f3)]
    for p in partners:
        pl.semaphore_signal(barrier, inc=1, device_id=p, device_id_type=mesh)
    pl.semaphore_wait(barrier, len(partners))
    spare = rows_n * slots
    mine = 1 - (top + row - 2 * top * row)
    kept = row * slots + g
    place = mine * kept + (1 - mine) * spare

    def copy(src, dst, n, device):
        return pltpu.make_async_remote_copy(
            src_ref=src, dst_ref=dst, send_sem=send.at[n], recv_sem=recv.at[n],
            device_id=device, device_id_type=mesh,
        )

    def unit(index, n, device):
        return copy(units.at[index], units.at[index], n, device)

    def at(which, shift):
        return (row if which == 0 else other) * slots + g + shift

    first = copy(l_ref, units.at[place], 0, (row, far))
    first.start()
    rights = copy(r_ref, rbuf.at[row], 2, (other, col))
    own = pltpu.make_async_copy(l_ref, units.at[place], local.at[0])
    own.start()
    own_right = pltpu.make_async_copy(r_ref, rbuf.at[row], local.at[1])
    own_right.start()
    across = copy(units.at[spare], units.at[kept], 1, (other, col))
    n1 = [unit(at(w, 0), 3 + w, (row, col + f1)) for w in range(2)]
    n2 = [[unit(at(w, s), 5 + 2 * w + m, (row, col + f2)) for m, s in enumerate((0, f1))] for w in range(2)]
    n3 = [
        [unit(at(w, s), 9 + 4 * w + m, (row, col + f3)) for m, s in enumerate((0, f1, f2, f1 + f2))]
        for w in range(2)
    ]
    own.wait()

    def spread():
        n1[0].start()
        n2[0][0].start()
        n3[0][0].start()

    @pl.when(mine == 1)
    def _():
        spread()

    @pl.when(mine == 0)
    def _():
        across.start()

    rights.start()
    for slot in range(slots if pad > res else 0):
        blank = slice(slot * pad + res, (slot + 1) * pad)
        lo_ref[:, blank, :] = jnp.zeros((2 * half, pad - res, lanes), BF)
    first.wait_recv()

    @pl.when(mine == 1)
    def _():
        across.start()

    @pl.when(mine == 0)
    def _():
        spread()

    across.wait_recv()
    n1[1].start()
    n2[1][0].start()
    n3[1][0].start()
    for w in range(2):
        n1[w].wait_recv()
        n2[w][1].start()
        n3[w][1].start()

    def halves(parts):
        low = jnp.concatenate([p[..., :seqs] for p in parts], axis=-1)
        high = jnp.concatenate([p[..., seqs:] for p in parts], axis=-1)
        return low, high

    def assemble(shift):
        slot = g + shift
        low, high = halves([units[d * slots + slot] for d in range(rows_n)])
        where = pl.ds(pl.multiple_of(slot * pad, pad), res)
        lo_ref[:half, where, :] = low
        lo_ref[half:, where, :] = high

    assemble(0)
    assemble(f1)
    own_right.wait()
    rights.wait_recv()
    low, high = halves([rbuf[d] for d in range(rows_n)])
    ro_ref[:, :half, :] = low
    ro_ref[:, half:, :] = high
    for m, s in enumerate((f2, f1 + f2)):
        for w in range(2):
            n2[w][m].wait_recv()
            n3[w][2 + m].start()
        assemble(s)
    for m, s in enumerate((0, f2, f1, f1 + f2)):
        for w in range(2):
            n3[w][m].wait_recv()
        assemble(f3 + s)
    for c in [first, across, rights, *n1, *n2[0], *n2[1], *n3[0], *n3[1]]:
        c.wait_send()


def gather_sides(left, right, slots, pad):
    half, res, lanes = left.shape
    return pl.pallas_call(
        functools.partial(gather_kernel, slots, pad),
        in_specs=[VM, VM],
        out_specs=(VM, VM),
        out_shape=(
            jax.ShapeDtypeStruct((2 * half, slots * pad, lanes), BF),
            jax.ShapeDtypeStruct((res, 2 * half, lanes), BF),
        ),
        scratch_shapes=[
            pltpu.VMEM((2 * slots + 1, half, res, lanes), BF),
            pltpu.VMEM((2, res, half, lanes), BF),
            pltpu.SemaphoreType.DMA((17,)),
            pltpu.SemaphoreType.DMA((17,)),
            pltpu.SemaphoreType.DMA((2,)),
        ],
        compiler_params=pltpu.CompilerParams(
            vmem_limit_bytes=16 << 20, collective_id=0, has_side_effects=True
        ),
        name="gather",
    )(left, right)


def join_kernel(rows_n, sizes, pad, *refs):
    count = rows_n * len(sizes)
    l_refs, r_refs = refs[:count], refs[count : count + rows_n]
    lo_ref, ro_ref = refs[count + rows_n :]
    half, res, lanes = l_refs[0].shape[1:]
    lo_ref[...] = jnp.zeros_like(lo_ref)
    seqs = lanes // 2

    def halves(parts):
        low = jnp.concatenate([p[..., :seqs] for p in parts], axis=-1)
        high = jnp.concatenate([p[..., seqs:] for p in parts], axis=-1)
        return low, high

    base = 0
    for stage, size in enumerate(sizes):
        for k in range(size):
            at = slice((base + k) * pad, (base + k) * pad + res)
            low, high = halves([l_refs[stage * rows_n + d][k] for d in range(rows_n)])
            lo_ref[:half, at, :] = low
            lo_ref[half:, at, :] = high
        base += size
    low, high = halves([r[...] for r in r_refs])
    ro_ref[:, :half, :] = low
    ro_ref[:, half:, :] = high


def pair_kernel(rows_n, patterns, l_s, r_s, sm_ref, rm_ref, rmv_ref, w_ref, out_ref, o_s, c_s):
    res, side, depth = r_s.shape
    slots = out_ref.shape[0] // res
    pad = l_s.shape[1] // slots
    row = lax.axis_index("row")
    col = lax.axis_index("col")
    local = lax.rem(col, slots)
    blocks = range(slots) if patterns is None else [jnp.bitwise_xor(local, p) for p in patterns]
    live_total = jnp.sum(sm_ref[...])
    rows_mask = pick(rmv_ref[...], row, slots * res, rows_n)
    gap = jnp.zeros((1, pad - res), jnp.int32)
    pieces = []
    for b in blocks:
        piece = pick(rows_mask, b, res, slots) if patterns else rows_mask[:, b * res : (b + 1) * res]
        pieces += [piece, gap] if pad > res else [piece]
    weights = w_ref[...].astype(F32).T.astype(BF)
    c_s[...] = jnp.concatenate(pieces, axis=1)
    step = o_s.shape[0]

    def group(n, carry):
        lhs = r_s[pl.ds(n * step, step)].reshape(step * side, depth)
        for a in range(side):
            block = nt(lhs, l_s[a]).astype(BF)
            o_s[:, a * side : (a + 1) * side, :] = block.reshape(step, side, slots * pad)
        for jj in range(step):
            j = n * step + jj
            live = live_total * rm_ref[col * res + j]
            counts = jnp.maximum(live * c_s[...], 1).astype(F32)
            flat = mm(weights, o_s[jj]) / counts
            rows = flat.T
            for k, b in enumerate(blocks):
                where = pl.ds(b * res if patterns is None else pl.multiple_of(b * res, res), res)
                out_ref[where, j, :] = rows[k * pad : k * pad + res]
        return carry

    lax.fori_loop(0, res // step, group, 0)


def shards(
    alignment, seq_mask, res_mask, attn_gain, outer_product_gain, w_query, w_key, w_value, w_gate,
    output_weight, w_left, w_right, w_pair,
):
    seqs, res, width = alignment.shape
    rows_n = lax.axis_size("row")
    cols_n = lax.axis_size("col")
    slots = cols_n // rows_n
    side = w_left.shape[1]
    half = side // 2
    sm = seq_mask.reshape(1, rows_n * seqs)
    pad = -(-res // 16) * 16
    gain = attn_gain.reshape(1, width)
    weights = (w_query, w_key, w_value, w_gate, output_weight)
    chunks = res // CHUNK
    parts = []
    for n in range(chunks):
        own = norm_chunk(alignment, gain, n)
        got = [own]
        for d in range(1, rows_n):
            perm = [((r + d) % rows_n, r) for r in range(rows_n)]
            got.append(lax.ppermute(own, "row", perm))
        parts.append(got)
    result = None
    for n in range(chunks):
        result = attend_chunk(parts[n], alignment, sm, weights, n, result)

    left, right = pl.pallas_call(
        functools.partial(sides_kernel, rows_n),
        in_specs=[VM, VM, VM, SM, VM, VM],
        out_specs=(VM, VM),
        out_shape=(
            jax.ShapeDtypeStruct((half, res, 2 * seqs), BF),
            jax.ShapeDtypeStruct((res, half, 2 * seqs), BF),
        ),
        scratch_shapes=[pltpu.VMEM((half, res, 2 * seqs), F32)],
        compiler_params=params(10 if rows_n == 2 else 24),
        name="sides",
    )(result, outer_product_gain.reshape(1, width), sm, res_mask, w_left.T, w_right.T)

    pair_rows = res * slots
    if rows_n == 2 and slots == 8:
        patterns = None
        left_all, right_all = gather_sides(left, right, slots, pad)
    else:
        rights = [right]
        for d in range(1, rows_n):
            perm = [((r + d) % rows_n, r) for r in range(rows_n)]
            rights.append(lax.ppermute(right, "row", perm))
        row = lax.axis_index("row")
        shift = lax.rem(lax.axis_index("col") // slots - row + rows_n, rows_n)
        stage = []
        for d in range(rows_n):
            unit = None
            for k in range(rows_n):
                if d == 0 and k == 0:
                    got = left
                else:
                    perm = [
                        (((r + d) % rows_n) * cols_n + r * slots + g, r * cols_n + ((r + k) % rows_n) * slots + g)
                        for r in range(rows_n)
                        for g in range(slots)
                    ]
                    got = lax.ppermute(left, ("row", "col"), perm)
                unit = got if unit is None else jnp.where(shift == k, got, unit)
            stage.append(unit[None])
        bits = [1 << n for n in range(slots.bit_length() - 1)]
        bits = bits[1:] + bits[:1]
        patterns = [0]
        sizes = [1]
        stages = [stage]
        for bit in bits:
            perm = [(c, c ^ bit) for c in range(cols_n)]
            fresh = []
            for d in range(rows_n):
                held = [s[d] for s in stages]
                sent = [lax.ppermute(h, "col", perm) for h in held]
                fresh.append(sent)
            patterns = patterns + [p ^ bit for p in patterns]
            for m in range(len(stages)):
                sizes.append(sizes[m])
                stages.append([fresh[d][m] for d in range(rows_n)])
        patterns = tuple(patterns)
        left_all, right_all = pl.pallas_call(
            functools.partial(join_kernel, rows_n, tuple(sizes), pad),
            in_specs=[VM] * (rows_n * len(sizes) + rows_n),
            out_specs=(VM, VM),
            out_shape=(
                jax.ShapeDtypeStruct((side, slots * pad, rows_n * seqs), BF),
                jax.ShapeDtypeStruct((res, side, rows_n * seqs), BF),
            ),
            compiler_params=params(48),
            name="join",
        )(*[u for s in stages for u in s], *rights)
    pair = pl.pallas_call(
        functools.partial(pair_kernel, rows_n, patterns),
        in_specs=[VM, VM, VM, SM, VM, VM],
        out_specs=VM,
        out_shape=jax.ShapeDtypeStruct((pair_rows, res, w_pair.shape[1]), F32),
        scratch_shapes=[
            pltpu.VMEM((CHUNK, side * side, slots * pad), BF),
            pltpu.VMEM((1, slots * pad), jnp.int32),
        ],
        compiler_params=params(24 if rows_n == 2 else 48),
        name="pairs",
    )(
        left_all, right_all, sm, res_mask,
        res_mask.reshape(1, cols_n * res), w_pair,
    )
    return (result, pair)


def solution(mesh):
    in_specs = (P("row", "col", None),) + (P(),) * 12
    out_specs = (P("row", "col", None), P("row", "col", None))
    return jax.shard_map(shards, mesh=mesh, in_specs=in_specs, out_specs=out_specs, check_vma=False)
```

```python
import functools

import jax
import jax.numpy as jnp
from jax import lax
from jax.experimental import pallas as pl
from jax.experimental.pallas import tpu as pltpu
from jax.sharding import PartitionSpec as P

HEAD_DIM = 32
LANES = 128
CHUNK = 8
PARTS = 2
BF = jnp.bfloat16
F32 = jnp.float32
VM = pl.BlockSpec(memory_space=pltpu.VMEM)
SM = pl.BlockSpec(memory_space=pltpu.SMEM)


def params(mib):
    return pltpu.CompilerParams(vmem_limit_bytes=mib << 20)


def pick(mask, index, width, count):
    value = mask[:, :width]
    for d in range(1, count):
        value = jnp.where(index == d, mask[:, d * width : (d + 1) * width], value)
    return value


def nt(a, b):
    return lax.dot_general(a, b, (((1,), (1,)), ((), ())), preferred_element_type=F32)


def mm(a, b):
    return jnp.dot(a, b, preferred_element_type=F32)


def norm_rows(values, gains):
    average = jnp.mean(values, -1, keepdims=True)
    centred = values - average
    spread = jnp.mean(centred * centred, -1, keepdims=True)
    return centred * lax.rsqrt(spread + 1e-05) * gains


def norm_kernel(seqs, res, x_ref, g_ref, o_ref):
    gains = g_ref[...]
    for r in range(CHUNK):
        rows = x_ref[:, r, :]
        o_ref[r] = norm_rows(rows, gains).astype(BF)


def norm_chunk(x, gain, chunk):
    seqs, res, width = x.shape
    return pl.pallas_call(
        functools.partial(norm_kernel, seqs, res),
        grid=(1,),
        in_specs=[
            pl.BlockSpec((seqs, CHUNK, width), lambda i: (0, chunk, 0)),
            pl.BlockSpec((1, width), lambda i: (0, 0)),
        ],
        out_specs=pl.BlockSpec((CHUNK, seqs, width), lambda i: (0, 0, 0)),
        out_shape=jax.ShapeDtypeStruct((CHUNK, seqs, width), BF),
        cost_estimate=pl.CostEstimate(flops=1 << 20, bytes_accessed=1 << 20, transcendentals=0),
        compiler_params=params(4),
        name="norm",
    )(x, gain)


def attend_kernel(rows_n, res, first, *refs):
    xs = refs[:rows_n]
    x_ref, sm_ref, rm_ref, gain_ref, wl_ref, wr_ref, wq, wk, wv, wg, wo = refs[rows_n : rows_n + 11]
    out_ref, l_ref, r_ref, q_s, k_s, v_s, g_s, l_s = refs[-8:]
    seqs, width = xs[0].shape[1], xs[0].shape[2]
    total = seqs * rows_n
    hidden = wq.shape[1]
    row = lax.axis_index("row")
    own = xs[0][...].reshape(CHUNK * seqs, width)
    q_s[...] = (mm(own, wq[...]) * (HEAD_DIM**-0.5)).astype(BF).reshape(CHUNK, seqs, hidden)
    g_s[...] = mm(own, wg[...]).reshape(CHUNK, seqs, hidden)
    for d in range(rows_n):
        part = xs[d][...].reshape(CHUNK * seqs, width)
        at = slice(d * seqs, (d + 1) * seqs)
        k_s[:, at, :] = mm(part, wk[...]).astype(BF).reshape(CHUNK, seqs, hidden)
        v_s[:, at, :] = mm(part, wv[...]).astype(BF).reshape(CHUNK, seqs, hidden)
    live = jnp.concatenate(
        [pick(sm_ref[...], lax.rem(row + d, rows_n), seqs, rows_n) for d in range(rows_n)], axis=1
    )
    bias = jnp.where(live > 0, 0.0, -1000000000.0).astype(F32)
    group = LANES // HEAD_DIM
    lane = lax.broadcasted_iota(jnp.int32, (seqs, LANES), 1) // HEAD_DIM
    ones = jnp.ones((total, LANES), BF)
    outs = []
    for r in range(CHUNK):
        halves = []
        for half in range(hidden // LANES):
            at = slice(half * LANES, (half + 1) * LANES)
            q = q_s[r, :, at]
            spread = jnp.concatenate(
                [jnp.where(lane == h, q, jnp.zeros_like(q)) for h in range(group)], axis=0
            )
            logits = nt(spread, k_s[r, :, at]) + bias
            peak = jnp.max(logits, axis=-1, keepdims=True)
            weights = jnp.exp(logits - peak).astype(BF)
            mixed = mm(weights, jnp.concatenate([v_s[r, :, at], ones], axis=1))
            top = mixed[:seqs, :LANES]
            den = mixed[:seqs, LANES:]
            for h in range(1, group):
                part = mixed[h * seqs : (h + 1) * seqs]
                top = jnp.where(lane == h, part[:, :LANES], top)
                den = jnp.where(lane == h, part[:, LANES:], den)
            halves.append((jax.nn.sigmoid(g_s[r, :, at]) * (top / den)).astype(BF))
        outs.append(jnp.concatenate(halves, axis=1))
    projected = mm(jnp.concatenate(outs, axis=0), wo[...])
    col = lax.axis_index("col")
    side = wl_ref.shape[0]
    half = side // 2
    seq_live = pick(sm_ref[...], row, seqs, rows_n).astype(F32)
    sides = jnp.concatenate([wl_ref[...], wr_ref[...]], axis=0)
    gains = gain_ref[...]
    for r in range(CHUNK):
        rows = x_ref[:, r, :] + projected[r * seqs : (r + 1) * seqs]
        out_ref[:, r, :] = rows
        second = norm_rows(rows, gains).astype(BF)
        both = nt(sides, second) * (seq_live * rm_ref[col * res + first + r].astype(F32))
        l_s[:, r, :] = jnp.concatenate([both[:half], both[half:side]], axis=1)
        r_ref[r] = jnp.concatenate([both[side : side + half], both[side + half :]], axis=1).astype(BF)
    l_ref[...] = l_s[...].astype(BF)


def attend_chunk(parts, x, sm, res_mask, weights, chunk, previous):
    rows_n = len(parts)
    seqs, res, width = x.shape
    total = seqs * rows_n
    hidden = weights[-1].shape[0]
    half = weights[1].shape[0] // 2

    block = pl.BlockSpec((seqs, CHUNK, width), lambda i: (0, chunk, 0))
    args = [*parts, x, sm, res_mask, *weights]
    specs = [VM] * rows_n + [block, VM, SM] + [VM] * len(weights)
    alias = {}
    if previous is not None:
        alias = {len(args): 0}
        args.append(previous)
        specs.append(pl.BlockSpec(memory_space=pl.ANY))
    tokens = CHUNK * total
    return pl.pallas_call(
        functools.partial(attend_kernel, rows_n, res, chunk * CHUNK),
        grid=(1,),
        in_specs=specs,
        out_specs=(block, VM, VM),
        out_shape=(
            jax.ShapeDtypeStruct(x.shape, F32),
            jax.ShapeDtypeStruct((half, CHUNK, 2 * seqs), BF),
            jax.ShapeDtypeStruct((CHUNK, half, 2 * seqs), BF),
        ),
        scratch_shapes=[
            pltpu.VMEM((CHUNK, seqs, hidden), BF),
            pltpu.VMEM((CHUNK, total, hidden), BF),
            pltpu.VMEM((CHUNK, total, hidden), BF),
            pltpu.VMEM((CHUNK, seqs, hidden), F32),
            pltpu.VMEM((half, CHUNK, 2 * seqs), F32),
        ],
        input_output_aliases=alias,
        cost_estimate=pl.CostEstimate(
            flops=tokens * width * hidden * 40, bytes_accessed=4 << 20, transcendentals=tokens * 8 * 64
        ),
        compiler_params=params(18 if rows_n == 2 else 48),
        name="attend",
    )(*args)


def gather_kernel(slots, pad, chunks, *refs):
    l_refs, r_refs = refs[:chunks], refs[chunks : 2 * chunks]
    lo_ref, ro_ref, units, rbuf, send, recv, local = refs[2 * chunks :]
    rows_n = 2
    half, res, lanes = units.shape[1:]
    seqs = lanes // 2
    row = lax.axis_index("row")
    col = lax.axis_index("col")
    top = col // slots
    g = lax.rem(col, slots)
    zl, x, core = lax.rem(col // 4, 2), lax.rem(col // 2, 2), lax.rem(col, 2)
    fx, fz = 2 * (1 - 2 * x), 4 * (1 - 2 * zl)
    f1 = (1 - core) * fx + core * fz
    f2 = core * fx + (1 - core) * fz
    f3 = 1 - 2 * core
    other = 1 - row
    far = col + slots * (1 - 2 * top)
    mesh = pl.DeviceIdType.MESH
    barrier = pltpu.get_barrier_semaphore()
    partners = [(row, far), (other, col), (row, col + f1), (row, col + f2), (row, col + f3)]
    for p in partners:
        pl.semaphore_signal(barrier, inc=1, device_id=p, device_id_type=mesh)
    pl.semaphore_wait(barrier, len(partners))
    spare = rows_n * slots
    mine = 1 - (top + row - 2 * top * row)
    kept = row * slots + g
    place = mine * kept + (1 - mine) * spare

    def copy(src, dst, n, device):
        return pltpu.make_async_remote_copy(
            src_ref=src, dst_ref=dst, send_sem=send.at[n], recv_sem=recv.at[n],
            device_id=device, device_id_type=mesh,
        )

    cut = half // PARTS

    def unit(src, dst, n, device):
        ends = [slice(p * cut, (p + 1) * cut) for p in range(PARTS)]
        return [copy(units.at[src, e], units.at[dst, e], n * PARTS + p, device) for p, e in enumerate(ends)]

    def same(index, n, device):
        return unit(index, index, n, device)

    def at(which, shift):
        return (row if which == 0 else other) * slots + g + shift

    mine_in = []
    for n in range(chunks):
        rows = pl.ds(n * CHUNK, CHUNK)
        mine_in.append(pltpu.make_async_copy(l_refs[n], units.at[place, :, rows], local.at[n]))
    own_right = [
        pltpu.make_async_copy(r_refs[n], rbuf.at[row, pl.ds(n * CHUNK, CHUNK)], local.at[chunks + n])
        for n in range(chunks)
    ]
    for c in mine_in + own_right:
        c.start()
    first = same(place, 0, (row, far))
    across = unit(spare, kept, 1, (other, col))
    rights = copy(rbuf.at[row], rbuf.at[row], 2 * PARTS, (other, col))
    n1 = [same(at(w, 0), 3 + w, (row, col + f1)) for w in range(2)]
    n2 = [[same(at(w, s), 5 + 2 * w + m, (row, col + f2)) for m, s in enumerate((0, f1))] for w in range(2)]
    n3 = [
        [same(at(w, s), 9 + 4 * w + m, (row, col + f3)) for m, s in enumerate((0, f1, f2, f1 + f2))]
        for w in range(2)
    ]
    for c in mine_in:
        c.wait()
    for p in range(PARTS):
        first[p].start()

    def spread(p):
        n1[0][p].start()
        n2[0][0][p].start()
        n3[0][0][p].start()

    @pl.when(mine == 1)
    def _():
        for p in range(PARTS):
            spread(p)

    @pl.when(mine == 0)
    def _():
        for p in range(PARTS):
            across[p].start()

    for c in own_right:
        c.wait()
    rights.start()
    for slot in range(slots if pad > res else 0):
        blank = slice(slot * pad + res, (slot + 1) * pad)
        lo_ref[:, blank, :] = jnp.zeros((2 * half, pad - res, lanes), BF)
    for p in range(PARTS):
        first[p].wait_recv()

        @pl.when(mine == 1)
        def _():
            across[p].start()

        @pl.when(mine == 0)
        def _():
            spread(p)

    for p in range(PARTS):
        across[p].wait_recv()
        n1[1][p].start()
        n2[1][0][p].start()
        n3[1][0][p].start()
    for w in range(2):
        for p in range(PARTS):
            n1[w][p].wait_recv()
            n2[w][1][p].start()
            n3[w][1][p].start()

    def halves(parts):
        low = jnp.concatenate([p[..., :seqs] for p in parts], axis=-1)
        high = jnp.concatenate([p[..., seqs:] for p in parts], axis=-1)
        return low, high

    def assemble(shift):
        slot = g + shift
        low, high = halves([units[d * slots + slot] for d in range(rows_n)])
        where = pl.ds(pl.multiple_of(slot * pad, pad), res)
        lo_ref[:half, where, :] = low
        lo_ref[half:, where, :] = high

    assemble(0)
    assemble(f1)
    rights.wait_recv()
    low, high = halves([rbuf[d] for d in range(rows_n)])
    ro_ref[:, :half, :] = low
    ro_ref[:, half:, :] = high
    for m, s in enumerate((f2, f1 + f2)):
        for w in range(2):
            for p in range(PARTS):
                n2[w][m][p].wait_recv()
                n3[w][2 + m][p].start()
        assemble(s)
    for m, s in enumerate((0, f2, f1, f1 + f2)):
        for w in range(2):
            for p in range(PARTS):
                n3[w][m][p].wait_recv()
        assemble(f3 + s)
    rights.wait_send()
    for c in [first, across, *n1, *n2[0], *n2[1], *n3[0], *n3[1]]:
        for p in range(PARTS):
            c[p].wait_send()


def gather_sides(lefts, rights, slots, pad):
    half, lanes = lefts[0].shape[0], lefts[0].shape[2]
    chunks = len(lefts)
    res = chunks * CHUNK
    return pl.pallas_call(
        functools.partial(gather_kernel, slots, pad, chunks),
        in_specs=[VM] * (2 * chunks),
        out_specs=(VM, VM),
        out_shape=(
            jax.ShapeDtypeStruct((2 * half, slots * pad, lanes), BF),
            jax.ShapeDtypeStruct((res, 2 * half, lanes), BF),
        ),
        scratch_shapes=[
            pltpu.VMEM((2 * slots + 1, half, res, lanes), BF),
            pltpu.VMEM((2, res, half, lanes), BF),
            pltpu.SemaphoreType.DMA((17 * PARTS,)),
            pltpu.SemaphoreType.DMA((17 * PARTS,)),
            pltpu.SemaphoreType.DMA((2 * chunks,)),
        ],
        compiler_params=pltpu.CompilerParams(
            vmem_limit_bytes=16 << 20, collective_id=0, has_side_effects=True
        ),
        name="gather",
    )(*lefts, *rights)


def join_kernel(rows_n, sizes, pad, *refs):
    count = rows_n * len(sizes)
    l_refs, r_refs = refs[:count], refs[count : count + rows_n]
    lo_ref, ro_ref = refs[count + rows_n :]
    half, res, lanes = l_refs[0].shape[1:]
    lo_ref[...] = jnp.zeros_like(lo_ref)
    seqs = lanes // 2

    def halves(parts):
        low = jnp.concatenate([p[..., :seqs] for p in parts], axis=-1)
        high = jnp.concatenate([p[..., seqs:] for p in parts], axis=-1)
        return low, high

    base = 0
    for stage, size in enumerate(sizes):
        for k in range(size):
            at = slice((base + k) * pad, (base + k) * pad + res)
            low, high = halves([l_refs[stage * rows_n + d][k] for d in range(rows_n)])
            lo_ref[:half, at, :] = low
            lo_ref[half:, at, :] = high
        base += size
    low, high = halves([r[...] for r in r_refs])
    ro_ref[:, :half, :] = low
    ro_ref[:, half:, :] = high


def pair_kernel(rows_n, patterns, l_s, r_s, sm_ref, rm_ref, rmv_ref, w_ref, out_ref, o_s, c_s):
    res, side, depth = r_s.shape
    slots = out_ref.shape[0] // res
    pad = l_s.shape[1] // slots
    row = lax.axis_index("row")
    col = lax.axis_index("col")
    local = lax.rem(col, slots)
    blocks = range(slots) if patterns is None else [jnp.bitwise_xor(local, p) for p in patterns]
    live_total = jnp.sum(sm_ref[...])
    rows_mask = pick(rmv_ref[...], row, slots * res, rows_n)
    gap = jnp.zeros((1, pad - res), jnp.int32)
    pieces = []
    for b in blocks:
        piece = pick(rows_mask, b, res, slots) if patterns else rows_mask[:, b * res : (b + 1) * res]
        pieces += [piece, gap] if pad > res else [piece]
    weights = w_ref[...].astype(F32).T.astype(BF)
    c_s[...] = jnp.concatenate(pieces, axis=1)
    step = o_s.shape[0]

    def group(n, carry):
        lhs = r_s[pl.ds(n * step, step)].reshape(step * side, depth)
        for a in range(side):
            block = nt(lhs, l_s[a]).astype(BF)
            o_s[:, a * side : (a + 1) * side, :] = block.reshape(step, side, slots * pad)
        for jj in range(step):
            j = n * step + jj
            live = live_total * rm_ref[col * res + j]
            counts = jnp.maximum(live * c_s[...], 1).astype(F32)
            flat = mm(weights, o_s[jj]) / counts
            rows = flat.T
            for k, b in enumerate(blocks):
                where = pl.ds(b * res if patterns is None else pl.multiple_of(b * res, res), res)
                out_ref[where, j, :] = rows[k * pad : k * pad + res]
        return carry

    lax.fori_loop(0, res // step, group, 0)


def shards(
    alignment, seq_mask, res_mask, attn_gain, outer_product_gain, w_query, w_key, w_value, w_gate,
    output_weight, w_left, w_right, w_pair,
):
    seqs, res, width = alignment.shape
    rows_n = lax.axis_size("row")
    cols_n = lax.axis_size("col")
    slots = cols_n // rows_n
    side = w_left.shape[1]
    half = side // 2
    sm = seq_mask.reshape(1, rows_n * seqs)
    pad = -(-res // 16) * 16
    gain = attn_gain.reshape(1, width)
    weights = (
        outer_product_gain.reshape(1, width), w_left.T, w_right.T,
        w_query, w_key, w_value, w_gate, output_weight,
    )
    chunks = res // CHUNK
    parts = []
    for n in range(chunks):
        own = norm_chunk(alignment, gain, n)
        got = [own]
        for d in range(1, rows_n):
            perm = [((r + d) % rows_n, r) for r in range(rows_n)]
            got.append(lax.ppermute(own, "row", perm))
        parts.append(got)
    result = None
    lefts, rights = [], []
    for n in range(chunks):
        result, left_part, right_part = attend_chunk(
            parts[n], alignment, sm, res_mask, weights, n, result
        )
        lefts.append(left_part)
        rights.append(right_part)

    pair_rows = res * slots
    if rows_n == 2 and slots == 8:
        patterns = None
        left_all, right_all = gather_sides(lefts, rights, slots, pad)
    else:
        left, right = jnp.concatenate(lefts, axis=1), jnp.concatenate(rights, axis=0)
        rights = [right]
        for d in range(1, rows_n):
            perm = [((r + d) % rows_n, r) for r in range(rows_n)]
            rights.append(lax.ppermute(right, "row", perm))
        row = lax.axis_index("row")
        shift = lax.rem(lax.axis_index("col") // slots - row + rows_n, rows_n)
        stage = []
        for d in range(rows_n):
            unit = None
            for k in range(rows_n):
                if d == 0 and k == 0:
                    got = left
                else:
                    perm = [
                        (((r + d) % rows_n) * cols_n + r * slots + g, r * cols_n + ((r + k) % rows_n) * slots + g)
                        for r in range(rows_n)
                        for g in range(slots)
                    ]
                    got = lax.ppermute(left, ("row", "col"), perm)
                unit = got if unit is None else jnp.where(shift == k, got, unit)
            stage.append(unit[None])
        bits = [1 << n for n in range(slots.bit_length() - 1)]
        bits = bits[1:] + bits[:1]
        patterns = [0]
        sizes = [1]
        stages = [stage]
        for bit in bits:
            perm = [(c, c ^ bit) for c in range(cols_n)]
            fresh = []
            for d in range(rows_n):
                held = [s[d] for s in stages]
                sent = [lax.ppermute(h, "col", perm) for h in held]
                fresh.append(sent)
            patterns = patterns + [p ^ bit for p in patterns]
            for m in range(len(stages)):
                sizes.append(sizes[m])
                stages.append([fresh[d][m] for d in range(rows_n)])
        patterns = tuple(patterns)
        left_all, right_all = pl.pallas_call(
            functools.partial(join_kernel, rows_n, tuple(sizes), pad),
            in_specs=[VM] * (rows_n * len(sizes) + rows_n),
            out_specs=(VM, VM),
            out_shape=(
                jax.ShapeDtypeStruct((side, slots * pad, rows_n * seqs), BF),
                jax.ShapeDtypeStruct((res, side, rows_n * seqs), BF),
            ),
            compiler_params=params(48),
            name="join",
        )(*[u for s in stages for u in s], *rights)
    pair = pl.pallas_call(
        functools.partial(pair_kernel, rows_n, patterns),
        in_specs=[VM, VM, VM, SM, VM, VM],
        out_specs=VM,
        out_shape=jax.ShapeDtypeStruct((pair_rows, res, w_pair.shape[1]), F32),
        scratch_shapes=[
            pltpu.VMEM((CHUNK, side * side, slots * pad), BF),
            pltpu.VMEM((1, slots * pad), jnp.int32),
        ],
        compiler_params=params(24 if rows_n == 2 else 48),
        name="pairs",
    )(
        left_all, right_all, sm, res_mask,
        res_mask.reshape(1, cols_n * res), w_pair,
    )
    return (result, pair)


def solution(mesh):
    in_specs = (P("row", "col", None),) + (P(),) * 12
    out_specs = (P("row", "col", None), P("row", "col", None))
    return jax.shard_map(shards, mesh=mesh, in_specs=in_specs, out_specs=out_specs, check_vma=False)
```

```python
import functools

import jax
import jax.numpy as jnp
from jax import lax
from jax.experimental import pallas as pl
from jax.experimental.pallas import tpu as pltpu
from jax.sharding import PartitionSpec as P

HEAD_DIM = 32
LANES = 128
CHUNK = 8
PARTS = 2
BF = jnp.bfloat16
F32 = jnp.float32
VM = pl.BlockSpec(memory_space=pltpu.VMEM)
SM = pl.BlockSpec(memory_space=pltpu.SMEM)


def params(mib):
    return pltpu.CompilerParams(vmem_limit_bytes=mib << 20)


def pick(mask, index, width, count):
    value = mask[:, :width]
    for d in range(1, count):
        value = jnp.where(index == d, mask[:, d * width : (d + 1) * width], value)
    return value


def nt(a, b):
    return lax.dot_general(a, b, (((1,), (1,)), ((), ())), preferred_element_type=F32)


def mm(a, b):
    return jnp.dot(a, b, preferred_element_type=F32)


def norm_rows(values, gains):
    average = jnp.mean(values, -1, keepdims=True)
    centred = values - average
    spread = jnp.mean(centred * centred, -1, keepdims=True)
    return centred * lax.rsqrt(spread + 1e-05) * gains


def norm_kernel(seqs, res, x_ref, g_ref, o_ref):
    gains = g_ref[...]
    for r in range(CHUNK):
        rows = x_ref[:, r, :]
        o_ref[r] = norm_rows(rows, gains).astype(BF)


def norm_chunk(x, gain, chunk):
    seqs, res, width = x.shape
    return pl.pallas_call(
        functools.partial(norm_kernel, seqs, res),
        grid=(1,),
        in_specs=[
            pl.BlockSpec((seqs, CHUNK, width), lambda i: (0, chunk, 0)),
            pl.BlockSpec((1, width), lambda i: (0, 0)),
        ],
        out_specs=pl.BlockSpec((CHUNK, seqs, width), lambda i: (0, 0, 0)),
        out_shape=jax.ShapeDtypeStruct((CHUNK, seqs, width), BF),
        cost_estimate=pl.CostEstimate(flops=1 << 20, bytes_accessed=1 << 20, transcendentals=0),
        compiler_params=params(4),
        name="norm",
    )(x, gain)


def attend_kernel(rows_n, res, first, *refs):
    xs = refs[:rows_n]
    x_ref, sm_ref, rm_ref, gain_ref, wl_ref, wr_ref, wq, wk, wv, wg, wo = refs[rows_n : rows_n + 11]
    out_ref, l_ref, r_ref, q_s, k_s, v_s, g_s, l_s = refs[-8:]
    seqs, width = xs[0].shape[1], xs[0].shape[2]
    total = seqs * rows_n
    hidden = wq.shape[1]
    row = lax.axis_index("row")
    own = xs[0][...].reshape(CHUNK * seqs, width)
    q_s[...] = (mm(own, wq[...]) * (HEAD_DIM**-0.5)).astype(BF).reshape(CHUNK, seqs, hidden)
    g_s[...] = mm(own, wg[...]).reshape(CHUNK, seqs, hidden)
    for d in range(rows_n):
        part = xs[d][...].reshape(CHUNK * seqs, width)
        at = slice(d * seqs, (d + 1) * seqs)
        k_s[:, at, :] = mm(part, wk[...]).astype(BF).reshape(CHUNK, seqs, hidden)
        v_s[:, at, :] = mm(part, wv[...]).astype(BF).reshape(CHUNK, seqs, hidden)
    live = jnp.concatenate(
        [pick(sm_ref[...], lax.rem(row + d, rows_n), seqs, rows_n) for d in range(rows_n)], axis=1
    )
    bias = jnp.where(live > 0, 0.0, -1000000000.0).astype(F32)
    group = LANES // HEAD_DIM
    lane = lax.broadcasted_iota(jnp.int32, (seqs, LANES), 1) // HEAD_DIM
    ones = jnp.ones((total, LANES), BF)
    outs = []
    for r in range(CHUNK):
        halves = []
        for half in range(hidden // LANES):
            at = slice(half * LANES, (half + 1) * LANES)
            q = q_s[r, :, at]
            spread = jnp.concatenate(
                [jnp.where(lane == h, q, jnp.zeros_like(q)) for h in range(group)], axis=0
            )
            logits = nt(spread, k_s[r, :, at]) + bias
            peak = jnp.max(logits, axis=-1, keepdims=True)
            weights = jnp.exp(logits - peak).astype(BF)
            mixed = mm(weights, jnp.concatenate([v_s[r, :, at], ones], axis=1))
            top = mixed[:seqs, :LANES]
            den = mixed[:seqs, LANES:]
            for h in range(1, group):
                part = mixed[h * seqs : (h + 1) * seqs]
                top = jnp.where(lane == h, part[:, :LANES], top)
                den = jnp.where(lane == h, part[:, LANES:], den)
            halves.append((jax.nn.sigmoid(g_s[r, :, at]) * (top / den)).astype(BF))
        outs.append(jnp.concatenate(halves, axis=1))
    projected = mm(jnp.concatenate(outs, axis=0), wo[...])
    col = lax.axis_index("col")
    side = wl_ref.shape[0]
    half = side // 2
    seq_live = pick(sm_ref[...], row, seqs, rows_n).astype(F32)
    sides = jnp.concatenate([wl_ref[...], wr_ref[...]], axis=0)
    gains = gain_ref[...]
    for r in range(CHUNK):
        rows = x_ref[:, r, :] + projected[r * seqs : (r + 1) * seqs]
        out_ref[:, r, :] = rows
        second = norm_rows(rows, gains).astype(BF)
        both = nt(sides, second) * (seq_live * rm_ref[col * res + first + r].astype(F32))
        l_s[:, r, :] = jnp.concatenate([both[:half], both[half:side]], axis=1)
        r_ref[r] = jnp.concatenate([both[side : side + half], both[side + half :]], axis=1).astype(BF)
    l_ref[...] = l_s[...].astype(BF)


def attend_chunk(parts, x, sm, res_mask, weights, chunk, previous):
    rows_n = len(parts)
    seqs, res, width = x.shape
    total = seqs * rows_n
    hidden = weights[-1].shape[0]
    half = weights[1].shape[0] // 2

    block = pl.BlockSpec((seqs, CHUNK, width), lambda i: (0, chunk, 0))
    args = [*parts, x, sm, res_mask, *weights]
    specs = [VM] * rows_n + [block, VM, SM] + [VM] * len(weights)
    alias = {}
    if previous is not None:
        alias = {len(args): 0}
        args.append(previous)
        specs.append(pl.BlockSpec(memory_space=pl.ANY))
    tokens = CHUNK * total
    return pl.pallas_call(
        functools.partial(attend_kernel, rows_n, res, chunk * CHUNK),
        grid=(1,),
        in_specs=specs,
        out_specs=(block, VM, VM),
        out_shape=(
            jax.ShapeDtypeStruct(x.shape, F32),
            jax.ShapeDtypeStruct((half, CHUNK, 2 * seqs), BF),
            jax.ShapeDtypeStruct((CHUNK, half, 2 * seqs), BF),
        ),
        scratch_shapes=[
            pltpu.VMEM((CHUNK, seqs, hidden), BF),
            pltpu.VMEM((CHUNK, total, hidden), BF),
            pltpu.VMEM((CHUNK, total, hidden), BF),
            pltpu.VMEM((CHUNK, seqs, hidden), F32),
            pltpu.VMEM((half, CHUNK, 2 * seqs), F32),
        ],
        input_output_aliases=alias,
        cost_estimate=pl.CostEstimate(
            flops=tokens * width * hidden * 40, bytes_accessed=4 << 20, transcendentals=tokens * 8 * 64
        ),
        compiler_params=params(18 if rows_n == 2 else 48),
        name="attend",
    )(*args)


def gather_kernel(slots, pad, chunks, *refs):
    l_refs, r_refs = refs[:chunks], refs[chunks : 2 * chunks]
    lo_ref, ro_ref, units, rbuf, send, recv, local = refs[2 * chunks :]
    rows_n = 2
    half, res, lanes = units.shape[1:]
    seqs = lanes // 2
    row = lax.axis_index("row")
    col = lax.axis_index("col")
    top = col // slots
    g = lax.rem(col, slots)
    zl, x, core = lax.rem(col // 4, 2), lax.rem(col // 2, 2), lax.rem(col, 2)
    fx, fz = 2 * (1 - 2 * x), 4 * (1 - 2 * zl)
    f1 = (1 - core) * fx + core * fz
    f2 = core * fx + (1 - core) * fz
    f3 = 1 - 2 * core
    other = 1 - row
    far = col + slots * (1 - 2 * top)
    mesh = pl.DeviceIdType.MESH
    barrier = pltpu.get_barrier_semaphore()
    partners = [(row, far), (other, col), (row, col + f1), (row, col + f2), (row, col + f3)]
    for p in partners:
        pl.semaphore_signal(barrier, inc=1, device_id=p, device_id_type=mesh)
    pl.semaphore_wait(barrier, len(partners))
    spare = rows_n * slots
    mine = 1 - (top + row - 2 * top * row)
    kept = row * slots + g
    place = mine * kept + (1 - mine) * spare

    def copy(src, dst, n, device):
        return pltpu.make_async_remote_copy(
            src_ref=src, dst_ref=dst, send_sem=send.at[n], recv_sem=recv.at[n],
            device_id=device, device_id_type=mesh,
        )

    cut = half // PARTS

    def unit(src, dst, n, device):
        ends = [slice(p * cut, (p + 1) * cut) for p in range(PARTS)]
        return [copy(units.at[src, e], units.at[dst, e], n * PARTS + p, device) for p, e in enumerate(ends)]

    def same(index, n, device):
        return unit(index, index, n, device)

    def at(which, shift):
        return (row if which == 0 else other) * slots + g + shift

    mine_in = []
    for n in range(chunks):
        rows = pl.ds(n * CHUNK, CHUNK)
        mine_in.append(pltpu.make_async_copy(l_refs[n], units.at[place, :, rows], local.at[n]))
    own_right = [
        pltpu.make_async_copy(r_refs[n], rbuf.at[row, pl.ds(n * CHUNK, CHUNK)], local.at[chunks + n])
        for n in range(chunks)
    ]
    for c in mine_in + own_right:
        c.start()
    first = same(place, 0, (row, far))
    across = unit(spare, kept, 1, (other, col))
    rights = copy(rbuf.at[row], rbuf.at[row], 2 * PARTS, (other, col))
    n1 = [same(at(w, 0), 3 + w, (row, col + f1)) for w in range(2)]
    n2 = [[same(at(w, s), 5 + 2 * w + m, (row, col + f2)) for m, s in enumerate((0, f1))] for w in range(2)]
    n3 = [
        [same(at(w, s), 9 + 4 * w + m, (row, col + f3)) for m, s in enumerate((0, f1, f2, f1 + f2))]
        for w in range(2)
    ]
    for c in mine_in:
        c.wait()
    for p in range(PARTS):
        first[p].start()

    def spread(p):
        n1[0][p].start()
        n2[0][0][p].start()
        n3[0][0][p].start()

    @pl.when(mine == 1)
    def _():
        for p in range(PARTS):
            spread(p)

    @pl.when(mine == 0)
    def _():
        for p in range(PARTS):
            across[p].start()

    for c in own_right:
        c.wait()
    rights.start()
    for slot in range(slots if pad > res else 0):
        blank = slice(slot * pad + res, (slot + 1) * pad)
        lo_ref[:, blank, :] = jnp.zeros((2 * half, pad - res, lanes), BF)
    for p in range(PARTS):
        first[p].wait_recv()

        @pl.when(mine == 1)
        def _():
            across[p].start()

        @pl.when(mine == 0)
        def _():
            spread(p)

    for p in range(PARTS):
        across[p].wait_recv()
        n1[1][p].start()
        n2[1][0][p].start()
        n3[1][0][p].start()
    for w in range(2):
        for p in range(PARTS):
            n1[w][p].wait_recv()
            n2[w][1][p].start()
            n3[w][1][p].start()

    def halves(parts):
        low = jnp.concatenate([p[..., :seqs] for p in parts], axis=-1)
        high = jnp.concatenate([p[..., seqs:] for p in parts], axis=-1)
        return low, high

    def assemble(shift):
        slot = g + shift
        low, high = halves([units[d * slots + slot] for d in range(rows_n)])
        where = pl.ds(pl.multiple_of(slot * pad, pad), res)
        lo_ref[:half, where, :] = low
        lo_ref[half:, where, :] = high

    assemble(0)
    assemble(f1)
    rights.wait_recv()
    low, high = halves([rbuf[d] for d in range(rows_n)])
    ro_ref[:, :half, :] = low
    ro_ref[:, half:, :] = high
    for m, s in enumerate((f2, f1 + f2)):
        for w in range(2):
            for p in range(PARTS):
                n2[w][m][p].wait_recv()
                n3[w][2 + m][p].start()
        assemble(s)
    for m, s in enumerate((0, f2, f1, f1 + f2)):
        for w in range(2):
            for p in range(PARTS):
                n3[w][m][p].wait_recv()
        assemble(f3 + s)
    rights.wait_send()
    for c in [first, across, *n1, *n2[0], *n2[1], *n3[0], *n3[1]]:
        for p in range(PARTS):
            c[p].wait_send()


def gather_sides(lefts, rights, slots, pad):
    half, lanes = lefts[0].shape[0], lefts[0].shape[2]
    chunks = len(lefts)
    res = chunks * CHUNK
    return pl.pallas_call(
        functools.partial(gather_kernel, slots, pad, chunks),
        in_specs=[VM] * (2 * chunks),
        out_specs=(VM, VM),
        out_shape=(
            jax.ShapeDtypeStruct((2 * half, slots * pad, lanes), BF),
            jax.ShapeDtypeStruct((res, 2 * half, lanes), BF),
        ),
        scratch_shapes=[
            pltpu.VMEM((2 * slots + 1, half, res, lanes), BF),
            pltpu.VMEM((2, res, half, lanes), BF),
            pltpu.SemaphoreType.DMA((17 * PARTS,)),
            pltpu.SemaphoreType.DMA((17 * PARTS,)),
            pltpu.SemaphoreType.DMA((2 * chunks,)),
        ],
        compiler_params=pltpu.CompilerParams(
            vmem_limit_bytes=16 << 20, collective_id=0, has_side_effects=True
        ),
        name="gather",
    )(*lefts, *rights)


def join_kernel(rows_n, sizes, pad, *refs):
    count = rows_n * len(sizes)
    l_refs, r_refs = refs[:count], refs[count : count + rows_n]
    lo_ref, ro_ref = refs[count + rows_n :]
    half, res, lanes = l_refs[0].shape[1:]
    lo_ref[...] = jnp.zeros_like(lo_ref)
    seqs = lanes // 2

    def halves(parts):
        low = jnp.concatenate([p[..., :seqs] for p in parts], axis=-1)
        high = jnp.concatenate([p[..., seqs:] for p in parts], axis=-1)
        return low, high

    base = 0
    for stage, size in enumerate(sizes):
        for k in range(size):
            at = slice((base + k) * pad, (base + k) * pad + res)
            low, high = halves([l_refs[stage * rows_n + d][k] for d in range(rows_n)])
            lo_ref[:half, at, :] = low
            lo_ref[half:, at, :] = high
        base += size
    low, high = halves([r[...] for r in r_refs])
    ro_ref[:, :half, :] = low
    ro_ref[:, half:, :] = high


def pair_kernel(rows_n, patterns, l_s, r_s, sm_ref, rm_ref, rmv_ref, w_ref, out_ref, o_s, c_s, w_s):
    res, side, depth = r_s.shape
    slots = out_ref.shape[0] // res
    pad = l_s.shape[1] // slots
    row = lax.axis_index("row")
    col = lax.axis_index("col")
    local = lax.rem(col, slots)
    blocks = range(slots) if patterns is None else [jnp.bitwise_xor(local, p) for p in patterns]
    live_total = jnp.sum(sm_ref[...])
    n = pl.program_id(0)
    rows_mask = pick(rmv_ref[...], row, slots * res, rows_n)
    gap = jnp.zeros((1, pad - res), jnp.int32)
    pieces = []
    for b in blocks:
        piece = pick(rows_mask, b, res, slots) if patterns else rows_mask[:, b * res : (b + 1) * res]
        pieces += [piece, gap] if pad > res else [piece]

    @pl.when(n == 0)
    def _():
        c_s[...] = jnp.concatenate(pieces, axis=1)
        w_s[...] = w_ref[...].astype(F32).T.astype(BF)

    step = o_s.shape[0]

    lhs = r_s[pl.ds(n * step, step)].reshape(step * side, depth)
    for a in range(side):
        block = nt(lhs, l_s[a]).astype(BF)
        o_s[:, a * side : (a + 1) * side, :] = block.reshape(step, side, slots * pad)
    for jj in range(step):
        j = n * step + jj
        live = live_total * rm_ref[col * res + j]
        counts = jnp.maximum(live * c_s[...], 1).astype(F32)
        flat = mm(w_s[...], o_s[jj]) * (1.0 / counts)
        rows = flat.T
        for k, b in enumerate(blocks):
            where = pl.ds(b * res if patterns is None else pl.multiple_of(b * res, res), res)
            out_ref[where, jj, :] = rows[k * pad : k * pad + res]


def shards(
    alignment, seq_mask, res_mask, attn_gain, outer_product_gain, w_query, w_key, w_value, w_gate,
    output_weight, w_left, w_right, w_pair,
):
    seqs, res, width = alignment.shape
    rows_n = lax.axis_size("row")
    cols_n = lax.axis_size("col")
    slots = cols_n // rows_n
    side = w_left.shape[1]
    half = side // 2
    sm = seq_mask.reshape(1, rows_n * seqs)
    pad = -(-res // 16) * 16
    gain = attn_gain.reshape(1, width)
    weights = (
        outer_product_gain.reshape(1, width), w_left.T, w_right.T,
        w_query, w_key, w_value, w_gate, output_weight,
    )
    chunks = res // CHUNK
    parts = []
    for n in range(chunks):
        own = norm_chunk(alignment, gain, n)
        got = [own]
        for d in range(1, rows_n):
            perm = [((r + d) % rows_n, r) for r in range(rows_n)]
            got.append(lax.ppermute(own, "row", perm))
        parts.append(got)
    result = None
    lefts, rights = [], []
    for n in range(chunks):
        result, left_part, right_part = attend_chunk(
            parts[n], alignment, sm, res_mask, weights, n, result
        )
        lefts.append(left_part)
        rights.append(right_part)

    pair_rows = res * slots
    if rows_n == 2 and slots == 8:
        patterns = None
        left_all, right_all = gather_sides(lefts, rights, slots, pad)
    else:
        left, right = jnp.concatenate(lefts, axis=1), jnp.concatenate(rights, axis=0)
        rights = [right]
        for d in range(1, rows_n):
            perm = [((r + d) % rows_n, r) for r in range(rows_n)]
            rights.append(lax.ppermute(right, "row", perm))
        row = lax.axis_index("row")
        shift = lax.rem(lax.axis_index("col") // slots - row + rows_n, rows_n)
        stage = []
        for d in range(rows_n):
            unit = None
            for k in range(rows_n):
                if d == 0 and k == 0:
                    got = left
                else:
                    perm = [
                        (((r + d) % rows_n) * cols_n + r * slots + g, r * cols_n + ((r + k) % rows_n) * slots + g)
                        for r in range(rows_n)
                        for g in range(slots)
                    ]
                    got = lax.ppermute(left, ("row", "col"), perm)
                unit = got if unit is None else jnp.where(shift == k, got, unit)
            stage.append(unit[None])
        bits = [1 << n for n in range(slots.bit_length() - 1)]
        bits = bits[1:] + bits[:1]
        patterns = [0]
        sizes = [1]
        stages = [stage]
        for bit in bits:
            perm = [(c, c ^ bit) for c in range(cols_n)]
            fresh = []
            for d in range(rows_n):
                held = [s[d] for s in stages]
                sent = [lax.ppermute(h, "col", perm) for h in held]
                fresh.append(sent)
            patterns = patterns + [p ^ bit for p in patterns]
            for m in range(len(stages)):
                sizes.append(sizes[m])
                stages.append([fresh[d][m] for d in range(rows_n)])
        patterns = tuple(patterns)
        left_all, right_all = pl.pallas_call(
            functools.partial(join_kernel, rows_n, tuple(sizes), pad),
            in_specs=[VM] * (rows_n * len(sizes) + rows_n),
            out_specs=(VM, VM),
            out_shape=(
                jax.ShapeDtypeStruct((side, slots * pad, rows_n * seqs), BF),
                jax.ShapeDtypeStruct((res, side, rows_n * seqs), BF),
            ),
            compiler_params=params(48),
            name="join",
        )(*[u for s in stages for u in s], *rights)
    pair = pl.pallas_call(
        functools.partial(pair_kernel, rows_n, patterns),
        grid=(res // CHUNK,),
        in_specs=[VM, VM, VM, SM, VM, VM],
        out_specs=pl.BlockSpec((pair_rows, CHUNK, w_pair.shape[1]), lambda n: (0, n, 0)),
        out_shape=jax.ShapeDtypeStruct((pair_rows, res, w_pair.shape[1]), F32),
        scratch_shapes=[
            pltpu.VMEM((CHUNK, side * side, slots * pad), BF),
            pltpu.VMEM((1, slots * pad), jnp.int32),
            pltpu.VMEM(w_pair.shape[::-1], BF),
        ],
        compiler_params=params(24 if rows_n == 2 else 48),
        name="pairs",
    )(
        left_all, right_all, sm, res_mask,
        res_mask.reshape(1, cols_n * res), w_pair,
    )
    return (result, pair)


def solution(mesh):
    in_specs = (P("row", "col", None),) + (P(),) * 12
    out_specs = (P("row", "col", None), P("row", "col", None))
    return jax.shard_map(shards, mesh=mesh, in_specs=in_specs, out_specs=out_specs, check_vma=False)
```
